256 devices in a mesh: row: 32 (over y_lo, z, core), col: 8 (over y_hi, x).
Axes of the slice: x: 4, y: 4 (y_hi: 2, y_lo: 2; y = y_hi * 2 + y_lo), z: 8, core: 2. Of those that a mesh axis runs over, the one named last changes fastest.
Arguments:
- alignment: bfloat16 [128, 1536, 256], P('row', 'col'), may hold values from -10 to 10
- alignment_norm_gain: float32 [256], replicated, may hold values from 0.1 to 1.9
- alignment_norm_bias: float32 [256], replicated, may hold values from -1.75 to 1.75
- projection_weight: bfloat16 [256, 64], replicated, may hold values from -0.375 to 0.375
- projection_bias_pair: float32 [64], replicated, may hold values from -3 to 3
- w_out: bfloat16 [1024, 128], replicated, may hold values from -0.1875 to 0.1875
- b_out: float32 [128], replicated, may hold values from -1.75 to 1.75
- pair_gain: float32 [128], replicated, may hold values from 0.1 to 1.9
- pair_bias: float32 [128], replicated, may hold values from -1.75 to 1.75
- w_up: bfloat16 [128, 512], replicated, may hold values from -0.5 to 0.5
- b_up: float32 [512], replicated, may hold values from -1.75 to 1.75
- w_down: bfloat16 [512, 128], replicated, may hold values from -0.25 to 0.25
- b_down: float32 [128], replicated, may hold values from -1.75 to 1.75
Outputs:
- pair_out: bfloat16 [1536, 1536, 128], P('row', 'col')
The draws below stay inside these ranges and needn't reach their ends.
All inputs are finite; a program needn't handle non-finite values.
Results may differ from the reference program's by a relative error of at most 0.0052.
Values may be sent and summed in bfloat16 or wider, within the bound.
A program may use at most 64 MiB of HBM per device.

```python
import jax
import jax.numpy as jnp
from jax import lax

CM = 256
C = 32
CZ = 128
CT = 512
I_DEV = 48
L = 1536
S = 128


def draw_alignment(key, part):
    common_key, noise_key = jax.random.split(jax.random.fold_in(key, 11))
    common = jax.random.normal(common_key, (1, L, CM), jnp.float32)
    noise_part = jax.random.normal(noise_key, (S, L, CM), jnp.float32)
    values = jnp.clip(common + noise_part, -10.0, 10.0)
    return values.astype(jnp.bfloat16)


def centred(rng, dims, spread, bound, kind=jnp.bfloat16):
    drawn = jax.random.normal(rng, dims, jnp.float32) * spread
    return jnp.minimum(jnp.maximum(drawn, -bound), bound).astype(kind)


def setup_inputs(seed: int = 0) -> dict:
    keys = jax.random.split(jax.random.key(seed), 14)
    alignment = draw_alignment(jax.random.fold_in(keys[13], 71), 0)
    alignment_norm_gain = jnp.clip(1.0 + 0.18 * jax.random.normal(keys[1], (CM,), jnp.float32), 0.1, 1.9)
    alignment_norm_bias = centred(keys[2], (CM,), 0.3, 1.75, jnp.float32)
    projection_weight = centred(keys[3], (CM, 2 * C), CM ** -0.5, 0.375)
    projection_bias_pair = centred(keys[4], (2 * C,), 0.5, 3.0, jnp.float32)
    w_out = centred(keys[5], (C * C, CZ), (C * C) ** -0.5, 0.1875)
    b_out = centred(keys[6], (CZ,), 0.3, 1.75, jnp.float32)
    pair_gain = jnp.clip(1.0 + 0.18 * jax.random.normal(keys[7], (CZ,), jnp.float32), 0.1, 1.9)
    pair_bias = centred(keys[8], (CZ,), 0.3, 1.75, jnp.float32)
    w_up = centred(keys[9], (CZ, CT), CZ ** -0.5, 0.5)
    b_up = centred(keys[10], (CT,), 0.3, 1.75, jnp.float32)
    w_down = centred(keys[11], (CT, CZ), CT ** -0.5, 0.25)
    b_down = centred(keys[12], (CZ,), 0.3, 1.75, jnp.float32)
    return {"alignment": alignment, "alignment_norm_gain": alignment_norm_gain, "alignment_norm_bias": alignment_norm_bias, "projection_weight": projection_weight, "projection_bias_pair": projection_bias_pair, "w_out": w_out, "b_out": b_out, "pair_gain": pair_gain, "pair_bias": pair_bias, "w_up": w_up, "b_up": b_up, "w_down": w_down, "b_down": b_down}


EPSILON = 1e-05

def layer_norm(values, gain_vec, bias_vec):
    average = lax.optimization_barrier(jnp.mean(values, axis=-1, keepdims=True))
    centered = values - average
    variance = lax.optimization_barrier(jnp.mean(centered * centered, axis=-1, keepdims=True))
    return centered * lax.rsqrt(variance + EPSILON) * gain_vec.astype(jnp.float32) + bias_vec.astype(jnp.float32)

def project(rows_in, alignment_norm_gain, alignment_norm_bias, projection_weight, projection_bias_pair):
    normed = layer_norm(rows_in.astype(jnp.float32), alignment_norm_gain, alignment_norm_bias).astype(jnp.bfloat16)
    return (jnp.dot(normed, projection_weight, preferred_element_type=jnp.float32) + projection_bias_pair).astype(jnp.bfloat16)

def finish(forward, mirror, w_out, b_out, pair_gain, pair_bias, w_up, b_up, w_down, b_down):
    forward_z = jnp.dot(forward, w_out, preferred_element_type=jnp.float32) + b_out
    mirror_z = jnp.dot(mirror, w_out, preferred_element_type=jnp.float32) + b_out
    pair = jax.nn.relu(forward_z) + jax.nn.relu(mirror_z)
    normed = layer_norm(pair, pair_gain, pair_bias).astype(jnp.bfloat16)
    hidden = jax.nn.relu(jnp.dot(normed, w_up, preferred_element_type=jnp.float32) + b_up).astype(jnp.bfloat16)
    return (pair + jnp.dot(hidden, w_down, preferred_element_type=jnp.float32) + b_down).astype(jnp.bfloat16)

def reference(alignment, alignment_norm_gain, alignment_norm_bias, projection_weight, projection_bias_pair, w_out, b_out, pair_gain, pair_bias, w_up, b_up, w_down, b_down):
    projected = project(alignment.reshape(S * L, CM), alignment_norm_gain, alignment_norm_bias, projection_weight, projection_bias_pair).reshape(S, L, 2 * C)
    left_all = projected[:, :, :C].astype(jnp.float32)
    right_all = projected[:, :, C:].astype(jnp.float32)

    def pair_block(block_index):
        first_row = (block_index * I_DEV).astype(jnp.int32)
        left_rows = lax.dynamic_slice_in_dim(left_all, first_row, I_DEV, 1)
        right_rows = lax.dynamic_slice_in_dim(right_all, first_row, I_DEV, 1)
        forward = (jnp.einsum('sia,sjb->ijab', left_rows, right_all) / S).astype(jnp.bfloat16)
        mirror = (jnp.einsum('sja,sib->ijab', left_all, right_rows) / S).astype(jnp.bfloat16)
        result = finish(forward.reshape(I_DEV * L, C * C), mirror.reshape(I_DEV * L, C * C), w_out, b_out, pair_gain, pair_bias, w_up, b_up, w_down, b_down)
        return result.reshape(I_DEV, L, CZ)
    blocks_out = lax.map(pair_block, jnp.arange(L // I_DEV, dtype=jnp.int32))
    return blocks_out.reshape(L, L, CZ)
```

```python
import functools

import jax
import jax.numpy as jnp
from jax import lax
from jax.experimental import pallas as pl
from jax.experimental.pallas import tpu as pltpu
from jax.sharding import PartitionSpec as P

EPSILON = 1e-05
VMEM_LIMIT = 60 * 1024 * 1024


def project_kernel(x_ref, gain_ref, bias_ref, w_ref, pbias_ref, x0_ref, x1_ref, y_ref, s0, s1, sy):
    rows = x_ref.shape[0]
    low = lax.broadcasted_iota(jnp.int32, (1, 128), 1) < 64
    w2 = jnp.concatenate([w_ref[...], w_ref[...]], axis=1)
    for s in range(rows):
        x = x_ref[s].astype(jnp.float32)
        mean = jnp.mean(x, axis=-1, keepdims=True)
        cen = x - mean
        var = jnp.mean(cen * cen, axis=-1, keepdims=True)
        normed = (cen * lax.rsqrt(var + EPSILON) * gain_ref[...] + bias_ref[...]).astype(jnp.bfloat16)
        d = jnp.dot(normed, w2, preferred_element_type=jnp.float32) + pbias_ref[...]
        for q in range(4):
            sy[q, :, s, :] = jnp.where(low, d[48 * q : 48 * q + 24], d[48 * q + 24 : 48 * q + 48])
        t0 = d[0:128].T
        s0[:, s, :] = t0[0:64]
        t1 = jnp.concatenate([d[128:192], d[128:192]], axis=0).T
        s1[0:16, s, :] = jnp.where(low, t1[0:16], t1[16:32])
        s1[16:32, s, :] = jnp.where(low, t1[32:48], t1[48:64])
    x0_ref[...] = s0[...].astype(jnp.bfloat16)
    x1_ref[...] = s1[...].astype(jnp.bfloat16)
    y_ref[...] = sy[...].astype(jnp.bfloat16)


def project(x, gain, bias, w, pbias):
    rows = x.shape[0]
    return pl.pallas_call(
        project_kernel,
        out_shape=(
            jax.ShapeDtypeStruct((64, rows, 128), jnp.bfloat16),
            jax.ShapeDtypeStruct((32, rows, 128), jnp.bfloat16),
            jax.ShapeDtypeStruct((4, 24, rows, 128), jnp.bfloat16),
        ),
        scratch_shapes=[
            pltpu.VMEM((64, rows, 128), jnp.float32),
            pltpu.VMEM((32, rows, 128), jnp.float32),
            pltpu.VMEM((4, 24, rows, 128), jnp.float32),
        ],
        name="project",
    )(x, gain[None, :], bias[None, :], w, jnp.concatenate([pbias, pbias])[None, :])


def pair_kernel(
    g0, g1, h, wf, wm, wup, wdn, bout, pg, pb, bup, bdn, out, lf, lm, r1f, r1m, pbuf
):
    step = pl.program_id(0)
    f32, bf16 = jnp.float32, jnp.bfloat16

    @pl.when(step == 0)
    def _():
        low = lax.broadcasted_iota(jnp.int32, (1, 128), 1) < 64
        for p in range(24):
            t = h[p].astype(f32).T.astype(bf16)
            rows = slice(p * 32, p * 32 + 32)
            lf[rows, 0:128] = t[0:32]
            lm[rows, 0:128] = t[32:64]
            lf[rows, 128:256] = t[64:96]
            lm[rows, 128:256] = t[96:128]
        zero = jnp.zeros((128, 128), f32)
        for dst, base in ((r1f, 16), (r1m, 0)):
            for b in range(16):
                q = g1[base + b].astype(f32)
                r = pltpu.roll(q, 64, axis=1)
                dst[b, 0:128] = jnp.where(low, q, zero).astype(bf16)
                dst[b, 128:256] = jnp.where(low, zero, r).astype(bf16)
                dst[b + 16, 0:128] = jnp.where(low, r, zero).astype(bf16)
                dst[b + 16, 128:256] = jnp.where(low, zero, q).astype(bf16)

    base = pl.multiple_of(step * 128, 128)
    for d, (lref, rref, off) in enumerate(((lf, r1f, 32), (lm, r1m, 0))):
        both = lref[pl.ds(base, 128), :]
        lhs0 = jnp.concatenate([both[:, 0:128], both[:, 128:256]], axis=0)
        for bp in range(16):
            b0, b1 = 2 * bp, 2 * bp + 1
            rhs0 = jnp.concatenate([g0[off + b0], g0[off + b1]], axis=1)
            o0 = jnp.dot(lhs0, rhs0, preferred_element_type=f32).astype(bf16)
            rhs1 = jnp.concatenate([rref[b0], rref[b1]], axis=1)
            o1 = jnp.dot(both, rhs1, preferred_element_type=f32).astype(bf16)
            for e, b in enumerate((b0, b1)):
                rows = slice(b * 32, b * 32 + 32)
                lanes = slice(e * 128, e * 128 + 128)
                for i in range(8):
                    pbuf[d, rows, i * 128 : i * 128 + 128] = o0[i * 32 : i * 32 + 32, lanes]
                for i in range(4):
                    pbuf[d, rows, (8 + i) * 128 : (9 + i) * 128] = o1[i * 32 : i * 32 + 32, lanes]

    for n in range(6):
        cols = slice(n * 256, n * 256 + 256)
        zf = jnp.dot(wf[...], pbuf[0, :, cols], preferred_element_type=f32)
        zm = jnp.dot(wm[...], pbuf[1, :, cols], preferred_element_type=f32)
        pair = jnp.maximum(zf + bout[...], 0.0) + jnp.maximum(zm + bout[...], 0.0)
        mean = jnp.mean(pair, axis=0, keepdims=True)
        cen = pair - mean
        var = jnp.mean(cen * cen, axis=0, keepdims=True)
        normed = (cen * lax.rsqrt(var + EPSILON) * pg[...] + pb[...]).astype(bf16)
        hid = jnp.dot(wup[...], normed, preferred_element_type=f32)
        hid = jnp.maximum(hid + bup[...], 0.0).astype(bf16)
        upd = jnp.dot(wdn[...], hid, preferred_element_type=f32)
        res = pair + upd + bdn[...]
        for e in range(2):
            g = 2 * n + e
            t = res[:, e * 128 : e * 128 + 128].T.astype(bf16)
            if g < 8:
                out[g // 4, g % 4, 0:128, :] = t
            else:
                out[0, g - 8, 128:192, :] = t[0:64]
                out[1, g - 8, 128:192, :] = t[64:128]


def pair_block(g0, g1, h, w_out, b_out, pair_gain, pair_bias, w_up, b_up, w_down, b_down):
    scaled = (w_out.astype(jnp.float32) / g0.shape[1]).astype(jnp.bfloat16)
    wf = scaled.reshape(32, 32, 128).transpose(2, 1, 0).reshape(128, 1024)
    wm = scaled.T
    whole = lambda shape: pl.BlockSpec(shape, lambda k: (0,) * len(shape), pipeline_mode=pl.Buffered(1))
    col = lambda v: v[:, None]
    args = (g0, g1, h, wf, wm, w_up.T, w_down.T, col(b_out), col(pair_gain), col(pair_bias), col(b_up), col(b_down))
    out = pl.pallas_call(
        pair_kernel,
        grid=(6,),
        in_specs=[whole(a.shape) for a in args],
        out_specs=pl.BlockSpec((2, 4, 192, 128), lambda k: (0, k, 0, 0)),
        out_shape=jax.ShapeDtypeStruct((2, 24, 192, 128), jnp.bfloat16),
        scratch_shapes=[
            pltpu.VMEM((768, 256), jnp.bfloat16),
            pltpu.VMEM((768, 256), jnp.bfloat16),
            pltpu.VMEM((32, 256, 128), jnp.bfloat16),
            pltpu.VMEM((32, 256, 128), jnp.bfloat16),
            pltpu.VMEM((2, 1024, 1536), jnp.bfloat16),
        ],
        compiler_params=pltpu.CompilerParams(vmem_limit_bytes=VMEM_LIMIT),
        name="pair",
    )(*args)
    return out.reshape(48, 192, 128)


def shards(
    alignment,
    alignment_norm_gain,
    alignment_norm_bias,
    projection_weight,
    projection_bias_pair,
    w_out,
    b_out,
    pair_gain,
    pair_bias,
    w_up,
    b_up,
    w_down,
    b_down,
):
    x0, x1, y = project(
        alignment, alignment_norm_gain, alignment_norm_bias, projection_weight, projection_bias_pair
    )
    g0 = lax.all_gather(x0, "row", axis=1, tiled=True)
    g1 = lax.all_gather(x1, "row", axis=1, tiled=True)
    wide = lax.all_gather(y, "col", axis=0, tiled=True)
    h = lax.all_to_all(wide, "row", split_axis=0, concat_axis=2, tiled=True)[0]
    return pair_block(
        g0, g1, h, w_out, b_out, pair_gain, pair_bias, w_up, b_up, w_down, b_down
    )


def solution(mesh):
    return jax.shard_map(
        shards,
        mesh=mesh,
        in_specs=(P("row", "col", None),) + (P(),) * 12,
        out_specs=P("row", "col", None),
        check_vma=False,
    )
```

```python
import functools

import jax
import jax.numpy as jnp
from jax import lax
from jax.experimental import pallas as pl
from jax.experimental.pallas import tpu as pltpu
from jax.sharding import PartitionSpec as P

EPSILON = 1e-05
VMEM_LIMIT = 60 * 1024 * 1024


MESH = pl.DeviceIdType.MESH
ZN, XN = 8, 4


def project_block(x_ref, gain_ref, bias_ref, w_ref, pbias_ref, stage):
    rows = x_ref.shape[0]
    low = lax.broadcasted_iota(jnp.int32, (1, 128), 1) < 64
    w2 = jnp.concatenate([w_ref[...], w_ref[...]], axis=1)
    for s in range(rows):
        x = x_ref[s].astype(jnp.float32)
        mean = jnp.mean(x, axis=-1, keepdims=True)
        cen = x - mean
        var = jnp.mean(cen * cen, axis=-1, keepdims=True)
        normed = (cen * lax.rsqrt(var + EPSILON) * gain_ref[...] + bias_ref[...]).astype(jnp.bfloat16)
        d = jnp.dot(normed, w2, preferred_element_type=jnp.float32) + pbias_ref[...]
        t0 = jnp.concatenate([d[48 * q : 48 * q + 32] for q in range(4)], axis=0).T
        t1 = jnp.concatenate([d[48 * q + 32 : 48 * q + 48] for q in range(4)] * 2, axis=0).T
        for h in range(2):
            stage[h, 0:32, s, :] = t0[32 * h : 32 * h + 32]
            stage[h, 32:48, s, :] = jnp.where(low, t1[32 * h : 32 * h + 16], t1[32 * h + 16 : 32 * h + 32])


def exchange_kernel(
    x_ref, gain_ref, bias_ref, w_ref, pbias_ref, g, hl, hr, stage, block, hstage, hsend,
    own_sem, l_send, l_recv, r_send, r_recv, y_send, y_recv, p_send, p_recv, h_send, h_recv,
):
    bf16, f32 = jnp.bfloat16, jnp.float32
    row, col = lax.axis_index("row"), lax.axis_index("col")
    core = lax.rem(row, 2)
    z = lax.rem(row // 2, ZN)
    ylo = row // (2 * ZN)
    x = lax.rem(col, XN)
    yhi = col // XN

    def row_of(ylo_, z_, core_):
        return (ylo_ * ZN + z_) * 2 + core_

    zup, zdn = lax.rem(z + 1, ZN), lax.rem(z + ZN - 1, ZN)
    up = (row_of(ylo, zup, core), col)
    down = (row_of(ylo, zdn, core), col)
    across = (row_of(1 - ylo, z, core), col)
    partner = (row_of(ylo, z, 1 - core), col)
    xup = (row, yhi * XN + lax.rem(x + 1, XN))
    xdn = (row, yhi * XN + lax.rem(x + XN - 1, XN))
    facing = (row_of(1 - ylo, z, core), (1 - yhi) * XN + x)

    barrier = pltpu.get_barrier_semaphore()
    others = (up, down, across, partner, xup, xdn, facing)
    for dev in others:
        pl.semaphore_signal(barrier, inc=1, device_id=dev, device_id_type=MESH)

    project_block(x_ref, gain_ref, bias_ref, w_ref, pbias_ref, stage)
    block[...] = stage[...].astype(bf16)
    own = [pltpu.make_async_copy(block.at[h], g.at[h, :, row], own_sem.at[h]) for h in range(2)]
    for c in own:
        c.start()
    pl.semaphore_wait(barrier, len(others))

    sent = []

    def slot(h, ylo_, dz, core_):
        return g.at[h, :, row_of(ylo_, lax.rem(z + dz + ZN, ZN), core_)]

    def copy(ref, send, recv, dev):
        c = pltpu.make_async_remote_copy(ref, ref, send, recv, device_id=dev, device_id_type=MESH)
        return c

    def send(ref, s, r, dev):
        c = copy(ref, s, r, dev)
        c.start()
        sent.append(c)

    def arrived(ref, r):
        copy(ref, own_sem.at[0], r, partner).wait_recv()

    def to_partner(h, which, dz, ylo_):
        send(slot(h, ylo_, dz, core), p_send.at[h, which, dz + 3], p_recv.at[h, which, dz + 3], partner)

    def ring_l(which, ylo_, dz):
        top, bottom = (4, 3) if which == 0 else (3, 4)
        ref = slot(0, ylo_, dz, core)
        if dz <= 0 and -dz < top:
            t = -dz
            send(ref, l_send.at[which, 0, t], l_recv.at[which, 0, t], up)
        if dz >= 0 and dz < bottom:
            t = dz
            send(ref, l_send.at[which, 1, t], l_recv.at[which, 1, t], down)

    def ring_r(dz):
        ref = slot(1, ylo, dz, core)
        if dz <= 0 and -dz < 4:
            send(ref, r_send.at[0, -dz], r_recv.at[0, -dz], up)
        if dz >= 0 and dz < 3:
            send(ref, r_send.at[1, dz], r_recv.at[1, dz], down)
        send(ref, y_send.at[1, dz + 4], y_recv.at[1, dz + 4], across)

    def pslot(h, which, ylo_, dz):
        i = (dz + 4) % 8
        send(slot(h, ylo_, dz, core), p_send.at[h, which, i], p_recv.at[h, which, i], partner)

    own[0].wait()
    own[1].wait()
    ring_l(0, ylo, 0)
    send(slot(0, ylo, 0, core), y_send.at[0, 0], y_recv.at[0, 0], across)
    ring_r(0)
    pslot(0, 0, ylo, 0)
    pslot(1, 0, ylo, 0)
    arrived(slot(0, 1 - ylo, 0, core), y_recv.at[0, 0])
    ring_l(1, 1 - ylo, 0)
    pslot(0, 1, 1 - ylo, 0)
    prev = [0]
    for t in range(1, 5):
        for which, ylo_ in ((0, ylo), (1, 1 - ylo)):
            top, bottom = (4, 3) if which == 0 else (3, 4)
            if t <= top:
                arrived(slot(0, ylo_, -t, core), l_recv.at[which, 0, t - 1])
                ring_l(which, ylo_, -t)
                pslot(0, which, ylo_, -t)
            if t <= bottom:
                arrived(slot(0, ylo_, t, core), l_recv.at[which, 1, t - 1])
                ring_l(which, ylo_, t)
                pslot(0, which, ylo_, t)
        now = []
        arrived(slot(1, ylo, -t, core), r_recv.at[0, t - 1])
        ring_r(-t)
        pslot(1, 0, ylo, -t)
        now.append(-t)
        if t <= 3:
            arrived(slot(1, ylo, t, core), r_recv.at[1, t - 1])
            ring_r(t)
            pslot(1, 0, ylo, t)
            now.append(t)
        for dz in prev:
            arrived(slot(1, 1 - ylo, dz, core), y_recv.at[1, dz + 4])
            pslot(1, 1, 1 - ylo, dz)
        prev = now
    for dz in prev:
        arrived(slot(1, 1 - ylo, dz, core), y_recv.at[1, dz + 4])
        pslot(1, 1, 1 - ylo, dz)

    offset = lax.rem(x - z // 2 + XN, XN)
    q = lax.rem(row, 4)
    shift0 = lax.rem(128 - 32 * q, 128)
    shift1 = lax.rem(128 - 32 * q + 64, 128)
    shift2 = lax.rem(128 - 16 * q + 32, 128)
    lane = lax.broadcasted_iota(jnp.int32, (1, 128), 1)
    flat = g.reshape(2, 48, 128, 128)
    for h, dst in ((0, hl), (1, hr)):
        for which in range(2):
            for dz in range(-3, 5):
                i = (dz + 4) % 8
                arrived(slot(h, (ylo, 1 - ylo)[which], dz if dz < 4 else -4, 1 - core), p_recv.at[h, which, i])

        @pl.when(offset == 0)
        def _(h=h, dst=dst):
            for p in range(16):
                a0 = pltpu.roll(flat[h, p].astype(f32), shift0, axis=1)
                a1 = pltpu.roll(flat[h, p + 16].astype(f32), shift1, axis=1)
                b = pltpu.roll(flat[h, 32 + p].astype(f32), shift2, axis=1)
                t = jnp.where(lane < 32, a0, jnp.where((lane >= 64) & (lane < 96), a1, b)).T
                for e in range(2):
                    at = pl.ds(p + 16 * e, 24, stride=32)
                    hstage[0, at, :] = t[64 * e : 64 * e + 24]
                    hstage[1, at, :] = t[64 * e + 24 : 64 * e + 48]
            hsend[h, :, 0:128] = hstage[0].astype(bf16)
            hsend[h, :, 128:256] = hstage[1].astype(bf16)

            @pl.when(ylo == yhi)
            def _():
                c = pltpu.make_async_copy(hsend.at[h], dst, h_recv.at[h])
                c.start()
                c.wait()

            @pl.when(ylo != yhi)
            def _():
                c = pltpu.make_async_remote_copy(
                    hsend.at[h], dst, h_send.at[h, 0], h_recv.at[h], device_id=facing, device_id_type=MESH
                )
                c.start()
                c.wait()

            copy(dst, h_send.at[h, 1], h_recv.at[h], xup).start()
            copy(dst, h_send.at[h, 2], h_recv.at[h], xdn).start()

        @pl.when(offset != 0)
        def _(h=h, dst=dst):
            arrived(dst, h_recv.at[h])

        relay, target = ((1, xup), (3, xdn))[h]

        @pl.when(offset == relay)
        def _(h=h, dst=dst, target=target):
            copy(dst, h_send.at[h, 3], h_recv.at[h], target).start()

    for h, dst in ((0, hl), (1, hr)):
        relay, target = ((1, xup), (3, xdn))[h]

        @pl.when(offset == 0)
        def _(h=h, dst=dst):
            copy(dst, h_send.at[h, 1], h_recv.at[h], xup).wait_send()
            copy(dst, h_send.at[h, 2], h_recv.at[h], xdn).wait_send()

        @pl.when(offset == relay)
        def _(h=h, dst=dst, target=target):
            copy(dst, h_send.at[h, 3], h_recv.at[h], target).wait_send()

    for c in sent:
        c.wait_send()


def exchange(x, gain, bias, w, pbias):
    rows = x.shape[0]
    bf16, f32 = jnp.bfloat16, jnp.float32
    vmem = pl.BlockSpec(memory_space=pltpu.VMEM)
    dma = pltpu.SemaphoreType.DMA
    return pl.pallas_call(
        exchange_kernel,
        in_specs=[vmem] * 5,
        out_specs=[vmem] * 3,
        out_shape=(
            jax.ShapeDtypeStruct((2, 48, 32, rows, 128), bf16),
            jax.ShapeDtypeStruct((768, 256), bf16),
            jax.ShapeDtypeStruct((768, 256), bf16),
        ),
        scratch_shapes=[
            pltpu.VMEM((2, 48, rows, 128), f32),
            pltpu.VMEM((2, 48, rows, 128), bf16),
            pltpu.VMEM((2, 768, 128), f32),
            pltpu.VMEM((2, 768, 256), bf16),
            dma((2,)),
            dma((2, 2, 4)),
            dma((2, 2, 4)),
            dma((2, 4)),
            dma((2, 4)),
            dma((2, 8)),
            dma((2, 8)),
            dma((2, 2, 8)),
            dma((2, 2, 8)),
            dma((2, 4)),
            dma((2,)),
        ],
        compiler_params=pltpu.CompilerParams(
            collective_id=0, has_side_effects=True, vmem_limit_bytes=16 * 1024 * 1024
        ),
        name="exchange",
    )(x, gain[None, :], bias[None, :], w, jnp.concatenate([pbias, pbias])[None, :])


def pair_kernel(
    g, lf, lm, wf, wm, wup, wdn, bout, pg, pb, bup, bdn, out, r1f, r1m, pbuf, zbuf, nbuf, hbuf, obuf,
    bout_b, pg_b, pb_b, bdn_b, bup_b, sem,
):
    f32, bf16 = jnp.float32, jnp.bfloat16
    low = lax.broadcasted_iota(jnp.int32, (1, 128), 1) < 64
    zero = jnp.zeros((128, 128), f32)
    for dst, base in ((r1f, 1), (r1m, 0)):
        for b in range(16):
            q = g[base, 32 + b].astype(f32)
            r = pltpu.roll(q, 64, axis=1)
            dst[b, 0:128] = jnp.where(low, q, zero).astype(bf16)
            dst[b, 128:256] = jnp.where(low, zero, r).astype(bf16)
            dst[b + 16, 0:128] = jnp.where(low, r, zero).astype(bf16)
            dst[b + 16, 128:256] = jnp.where(low, zero, q).astype(bf16)
    for wide, narrow in ((bout_b, bout), (pg_b, pg), (pb_b, pb), (bdn_b, bdn), (bup_b, bup)):
        wide[...] = jnp.broadcast_to(narrow[...], wide.shape)

    def twice(ref, rows=slice(None)):
        v = ref[rows, :]
        return jnp.concatenate([v, v], axis=1)

    def outer_unit(k, d, bp):
        lref, rref, half = ((lf, r1f, 1), (lm, r1m, 0))[d]
        both = lref[pl.ds(pl.multiple_of(k * 128, 128), 128), :]
        lhs0 = jnp.concatenate([both[:, 0:128], both[:, 128:256]], axis=0)
        b0, b1 = 2 * bp, 2 * bp + 1
        rhs0 = jnp.concatenate([g[half, b0], g[half, b1]], axis=1)
        o0 = jnp.dot(lhs0, rhs0, preferred_element_type=f32).astype(bf16)
        rhs1 = jnp.concatenate([rref[b0], rref[b1]], axis=1)
        o1 = jnp.dot(both, rhs1, preferred_element_type=f32).astype(bf16)
        for e, b in enumerate((b0, b1)):
            rows = slice(b * 32, b * 32 + 32)
            lanes = slice(e * 128, e * 128 + 128)
            for i in range(8):
                pbuf[d, rows, i * 128 : i * 128 + 128] = o0[i * 32 : i * 32 + 32, lanes]
            for i in range(4):
                pbuf[d, rows, (8 + i) * 128 : (9 + i) * 128] = o1[i * 32 : i * 32 + 32, lanes]

    def project_chunk(n):
        cols = slice(n * 256, n * 256 + 256)
        b = twice(bout_b)
        zf = jnp.dot(wf[...], pbuf[0, :, cols], preferred_element_type=f32)
        zm = jnp.dot(wm[...], pbuf[1, :, cols], preferred_element_type=f32)
        zbuf[:, cols] = jnp.maximum(zf + b, 0.0) + jnp.maximum(zm + b, 0.0)

    def norm_chunk(n):
        pair = zbuf[:, n * 256 : n * 256 + 256]
        mean = jnp.mean(pair, axis=0, keepdims=True)
        cen = pair - mean
        var = jnp.mean(cen * cen, axis=0, keepdims=True)
        nbuf[n % 2] = (cen * lax.rsqrt(var + EPSILON) * twice(pg_b) + twice(pb_b)).astype(bf16)

    def up_chunk(n, part):
        rows = slice(part * 128, part * 128 + 128)
        hid = jnp.dot(wup[rows, :], nbuf[n % 2], preferred_element_type=f32)
        hbuf[n % 2, rows, :] = jnp.maximum(hid + twice(bup_b, rows), 0.0).astype(bf16)

    def down_chunk(n, slot):
        upd = jnp.dot(wdn[...], hbuf[n % 2], preferred_element_type=f32)
        res = zbuf[:, n * 256 : n * 256 + 256] + upd + twice(bdn_b)
        for e in range(2):
            c = 2 * n + e
            t = res[:, e * 128 : e * 128 + 128].T.astype(bf16)
            for q in range(4):
                if c < 8:
                    obuf[slot, c // 4, c % 4, 48 * q : 48 * q + 32, :] = t[32 * q : 32 * q + 32]
                else:
                    obuf[slot, 0, c - 8, 48 * q + 32 : 48 * q + 48, :] = t[16 * q : 16 * q + 16]
                    obuf[slot, 1, c - 8, 48 * q + 32 : 48 * q + 48, :] = t[64 + 16 * q : 80 + 16 * q]

    def transition(slot):
        stages = []
        for n in range(6):
            stages.append(functools.partial(norm_chunk, n))
            for part in range(4):
                stages.append(functools.partial(up_chunk, n, part))
            stages.append(functools.partial(down_chunk, n, slot))
        return stages

    def outer(k):
        return [functools.partial(outer_unit, k, d, bp) for d in range(2) for bp in range(16)]

    def store(k, slot):
        return [
            pltpu.make_async_copy(obuf.at[slot, w], out.at[w, pl.ds(4 * k, 4)], sem.at[slot, w])
            for w in range(2)
        ]

    for unit in outer(0):
        unit()
    for n in range(6):
        project_chunk(n)

    def body(k, carry):
        slot = lax.rem(k + 1, 2)

        @pl.when(k >= 3)
        def _():
            for c in store(k - 3, slot):
                c.wait()

        units, stages = outer(k), transition(slot)
        done = 0
        for i, unit in enumerate(units):
            unit()
            while done < (i + 1) * len(stages) // len(units):
                stages[done]()
                done += 1
        for c in store(k - 1, slot):
            c.start()
        for n in range(6):
            project_chunk(n)
        return carry

    lax.fori_loop(1, 6, body, 0)
    for c in store(3, 1):
        c.wait()
    for stage in transition(1):
        stage()
    for c in store(5, 1):
        c.start()
    for k, slot in ((4, 0), (5, 1)):
        for c in store(k, slot):
            c.wait()


def pair_block(g, hl, hr, w_out, b_out, pair_gain, pair_bias, w_up, b_up, w_down, b_down):
    bf16, f32 = jnp.bfloat16, jnp.float32
    scaled = (w_out.astype(jnp.float32) / g.shape[2]).astype(jnp.bfloat16)
    wf = scaled.reshape(32, 32, 128).transpose(2, 1, 0).reshape(128, 1024)
    wm = scaled.T
    col = lambda v: v[:, None]
    args = (g, hl, hr, wf, wm, w_up.T, w_down.T, col(b_out), col(pair_gain), col(pair_bias), col(b_up), col(b_down))
    out = pl.pallas_call(
        pair_kernel,
        in_specs=[pl.BlockSpec(memory_space=pltpu.VMEM) for a in args],
        out_specs=pl.BlockSpec(memory_space=pl.ANY),
        out_shape=jax.ShapeDtypeStruct((2, 24, 192, 128), jnp.bfloat16),
        scratch_shapes=[
            pltpu.VMEM((32, 256, 128), bf16),
            pltpu.VMEM((32, 256, 128), bf16),
            pltpu.VMEM((2, 1024, 1536), bf16),
            pltpu.VMEM((128, 1536), f32),
            pltpu.VMEM((2, 128, 256), bf16),
            pltpu.VMEM((2, 512, 256), bf16),
            pltpu.VMEM((2, 2, 4, 192, 128), bf16),
            pltpu.VMEM((128, 128), f32),
            pltpu.VMEM((128, 128), f32),
            pltpu.VMEM((128, 128), f32),
            pltpu.VMEM((128, 128), f32),
            pltpu.VMEM((512, 128), f32),
            pltpu.SemaphoreType.DMA((2, 2)),
        ],
        compiler_params=pltpu.CompilerParams(vmem_limit_bytes=VMEM_LIMIT),
        name="pair",
    )(*args)
    return out.reshape(48, 192, 128)


def shards(
    alignment,
    alignment_norm_gain,
    alignment_norm_bias,
    projection_weight,
    projection_bias_pair,
    w_out,
    b_out,
    pair_gain,
    pair_bias,
    w_up,
    b_up,
    w_down,
    b_down,
):
    g, hl, hr = exchange(
        alignment, alignment_norm_gain, alignment_norm_bias, projection_weight, projection_bias_pair
    )
    g = g.reshape(2, 48, 128, 128)
    return pair_block(
        g, hl, hr, w_out, b_out, pair_gain, pair_bias, w_up, b_up, w_down, b_down
    )


def solution(mesh):
    return jax.shard_map(
        shards,
        mesh=mesh,
        in_specs=(P("row", "col", None),) + (P(),) * 12,
        out_specs=P("row", "col", None),
        check_vma=False,
    )
```

```python
import functools

import jax
import jax.numpy as jnp
from jax import lax
from jax.experimental import pallas as pl
from jax.experimental.pallas import tpu as pltpu
from jax.sharding import PartitionSpec as P

EPSILON = 1e-05
VMEM_LIMIT = 60 * 1024 * 1024


MESH = pl.DeviceIdType.MESH
ZN, XN = 8, 4


def project_block(x_ref, gain_ref, bias_ref, w_ref, pbias_ref, stage):
    rows = x_ref.shape[0]
    low = lax.broadcasted_iota(jnp.int32, (1, 128), 1) < 64
    w2 = jnp.concatenate([w_ref[...], w_ref[...]], axis=0)
    pbias = jnp.concatenate([pbias_ref[...], pbias_ref[...]], axis=1)
    for s in range(rows):
        x = x_ref[s].astype(jnp.float32)
        mean = jnp.mean(x, axis=-1, keepdims=True)
        cen = x - mean
        var = jnp.mean(cen * cen, axis=-1, keepdims=True)
        normed = (cen * lax.rsqrt(var + EPSILON) * gain_ref[...] + bias_ref[...]).astype(jnp.bfloat16)
        d = lax.dot_general(normed, w2, (((1,), (1,)), ((), ())), preferred_element_type=jnp.float32)
        d = d + pbias
        t0 = jnp.concatenate([d[48 * q : 48 * q + 32] for q in range(4)], axis=0).T
        t1 = jnp.concatenate([d[48 * q + 32 : 48 * q + 48] for q in range(4)] * 2, axis=0).T
        for h in range(2):
            stage[h, 0:32, s, :] = t0[32 * h : 32 * h + 32]
            stage[h, 32:48, s, :] = jnp.where(low, t1[32 * h : 32 * h + 16], t1[32 * h + 16 : 32 * h + 32])


def fused_kernel(
    x_ref, gain_ref, bias_ref, w_ref, pbias_ref, w_out, bout, pg, pb, w_up, bup, w_down, bdn, out,
    g, hl, hr, stage, block, hstage, hsend, r1f, r1m, pbuf, zbuf, nbuf, hbuf, wtmp,
    wf, wm, wup, wdn, bout_b, pg_b, pb_b, bdn_b, bup_b,
    own_sem, l_send, l_recv, r_send, r_recv, y_send, y_recv, p_send, p_recv, hs_sem, hf_sem, h_recv,
):
    bf16, f32 = jnp.bfloat16, jnp.float32

    def prepare_weights():
        total = 4 * 32
        wtmp[...] = w_out[...].astype(f32) * (1.0 / total)
        for m in range(8):
            rows = slice(m * 128, m * 128 + 128)
            wm[:, rows] = wtmp[rows, :].T.astype(bf16)
            picked = [wtmp[pl.ds(4 * m + e, 32, stride=32), :] for e in range(4)]
            wf[:, rows] = jnp.concatenate(picked, axis=0).T.astype(bf16)
        for m in range(4):
            rows = slice(m * 128, m * 128 + 128)
            wup[rows, :] = w_up[:, rows].astype(f32).T.astype(bf16)
            wdn[:, rows] = w_down[rows, :].astype(f32).T.astype(bf16)
            bup_b[rows, :] = jnp.broadcast_to(bup[:, rows], (128, 128)).T
        for wide, narrow in ((bout_b, bout), (pg_b, pg), (pb_b, pb), (bdn_b, bdn)):
            wide[...] = jnp.broadcast_to(narrow[...], (128, 128)).T

    row, col = lax.axis_index("row"), lax.axis_index("col")
    core = lax.rem(row, 2)
    z = lax.rem(row // 2, ZN)
    ylo = row // (2 * ZN)
    x = lax.rem(col, XN)
    yhi = col // XN

    def row_of(ylo_, z_, core_):
        return (ylo_ * ZN + z_) * 2 + core_

    zup, zdn = lax.rem(z + 1, ZN), lax.rem(z + ZN - 1, ZN)
    up = (row_of(ylo, zup, core), col)
    down = (row_of(ylo, zdn, core), col)
    across = (row_of(1 - ylo, z, core), col)
    partner = (row_of(ylo, z, 1 - core), col)
    xup = (row, yhi * XN + lax.rem(x + 1, XN))
    xdn = (row, yhi * XN + lax.rem(x + XN - 1, XN))
    facing = (row_of(1 - ylo, z, core), (1 - yhi) * XN + x)

    barrier = pltpu.get_barrier_semaphore()
    others = (up, down, across, partner, xup, xdn, facing)
    for dev in others:
        pl.semaphore_signal(barrier, inc=1, device_id=dev, device_id_type=MESH)

    project_block(x_ref, gain_ref, bias_ref, w_ref, pbias_ref, stage)
    block[...] = stage[...].astype(bf16)
    own = [pltpu.make_async_copy(block.at[h], g.at[h, :, row], own_sem.at[h]) for h in range(2)]
    for c in own:
        c.start()
    pl.semaphore_wait(barrier, len(others))

    sent = []

    def slot(h, ylo_, dz, core_):
        return g.at[h, :, row_of(ylo_, lax.rem(z + dz + ZN, ZN), core_)]

    def copy(ref, send, recv, dev):
        c = pltpu.make_async_remote_copy(ref, ref, send, recv, device_id=dev, device_id_type=MESH)
        return c

    def send(ref, s, r, dev):
        c = copy(ref, s, r, dev)
        c.start()
        sent.append(c)

    def arrived(ref, r):
        copy(ref, own_sem.at[0], r, partner).wait_recv()

    def ring_l(which, ylo_, dz):
        top, bottom = (4, 3) if which == 0 else (3, 4)
        ref = slot(0, ylo_, dz, core)
        if dz <= 0 and -dz < top:
            t = -dz
            send(ref, l_send.at[which, 0, t], l_recv.at[which, 0, t], up)
        if dz >= 0 and dz < bottom:
            t = dz
            send(ref, l_send.at[which, 1, t], l_recv.at[which, 1, t], down)

    def ring_r(dz):
        ref = slot(1, ylo, dz, core)
        if dz <= 0 and -dz < 4:
            send(ref, r_send.at[0, -dz], r_recv.at[0, -dz], up)
        if dz >= 0 and dz < 3:
            send(ref, r_send.at[1, dz], r_recv.at[1, dz], down)
        send(ref, y_send.at[1, dz + 4], y_recv.at[1, dz + 4], across)

    def pslot(h, which, ylo_, dz):
        i = (dz + 4) % 8
        send(slot(h, ylo_, dz, core), p_send.at[h, which, i], p_recv.at[h, which, i], partner)

    own[0].wait()
    own[1].wait()
    ring_l(0, ylo, 0)
    send(slot(0, ylo, 0, core), y_send.at[0, 0], y_recv.at[0, 0], across)
    ring_r(0)
    pslot(0, 0, ylo, 0)
    pslot(1, 0, ylo, 0)
    prepare_weights()
    arrived(slot(0, 1 - ylo, 0, core), y_recv.at[0, 0])
    ring_l(1, 1 - ylo, 0)
    pslot(0, 1, 1 - ylo, 0)
    prev = [0]
    for t in range(1, 5):
        for dz in (-t, t):
            if dz == 4:
                continue
            way = 0 if dz < 0 else 1
            arrived(slot(0, ylo, dz, core), l_recv.at[0, way, t - 1])
            ring_l(0, ylo, dz)
            arrived(slot(1, ylo, dz, core), r_recv.at[way, t - 1])
            ring_r(dz)
            pslot(0, 0, ylo, dz)
            pslot(1, 0, ylo, dz)
        for dz in (-t, t):
            if dz == -4:
                continue
            way = 0 if dz < 0 else 1
            arrived(slot(0, 1 - ylo, dz, core), l_recv.at[1, way, t - 1])
            ring_l(1, 1 - ylo, dz)
            pslot(0, 1, 1 - ylo, dz)
        for dz in prev:
            arrived(slot(1, 1 - ylo, dz, core), y_recv.at[1, dz + 4])
            pslot(1, 1, 1 - ylo, dz)
        prev = [dz for dz in (-t, t) if dz != 4]
    for dz in prev:
        arrived(slot(1, 1 - ylo, dz, core), y_recv.at[1, dz + 4])
        pslot(1, 1, 1 - ylo, dz)

    offset = lax.rem(x - z // 2 + XN, XN)
    q = lax.rem(row, 4)
    shift0 = lax.rem(128 - 32 * q, 128)
    shift1 = lax.rem(128 - 32 * q + 64, 128)
    shift2 = lax.rem(128 - 16 * q + 32, 128)
    lane = lax.broadcasted_iota(jnp.int32, (1, 128), 1)
    flat = g.reshape(2, 48, 128, 128)
    self_source = (offset == 0) & (ylo == yhi)
    far_source = (offset == 0) & (ylo != yhi)

    def chunk(ref, k):
        return ref.at[pl.ds(pl.multiple_of(k * 128, 128), 128)]

    def local(h, dst, k):
        return pltpu.make_async_copy(chunk(hsend.at[h], k), chunk(dst, k), h_recv.at[h, k])

    def first(h, dst, k):
        return pltpu.make_async_remote_copy(
            chunk(hsend.at[h], k), chunk(dst, k), hs_sem.at[h, k], h_recv.at[h, k], device_id=facing, device_id_type=MESH
        )

    def onward(h, dst, k, way):
        return copy(chunk(dst, k), hf_sem.at[h, way, k], h_recv.at[h, k], (xup, xdn)[way])

    def make_rows(h, dst):
        for p in range(16):
            a0 = pltpu.roll(flat[h, p].astype(f32), shift0, axis=1)
            a1 = pltpu.roll(flat[h, p + 16].astype(f32), shift1, axis=1)
            b = pltpu.roll(flat[h, 32 + p].astype(f32), shift2, axis=1)
            t = jnp.where(lane < 32, a0, jnp.where((lane >= 64) & (lane < 96), a1, b)).T
            for e in range(2):
                at = pl.ds(p + 16 * e, 24, stride=32)
                hstage[0, at, :] = t[64 * e : 64 * e + 24]
                hstage[1, at, :] = t[64 * e + 24 : 64 * e + 48]
        hsend[h, :, 0:128] = hstage[0].astype(bf16)
        hsend[h, :, 128:256] = hstage[1].astype(bf16)

        @pl.when(ylo == yhi)
        def _():
            for k in range(6):
                local(h, dst, k).start()

        @pl.when(ylo != yhi)
        def _():
            for k in range(6):
                first(h, dst, k).start()

    def onward_root(h, dst, k):
        @pl.when(offset == 0)
        def _():
            local(h, dst, k).wait()
            onward(h, dst, k, 0).start()
            onward(h, dst, k, 1).start()

    def onward_side(h, dst, k):
        @pl.when((offset == 1) | (offset == 3))
        def _():
            local(h, dst, k).wait()

        @pl.when((offset == 1) & (lax.rem(k, 2) == 0))
        def _():
            onward(h, dst, k, 0).start()

        @pl.when((offset == 3) & (lax.rem(k, 2) == 1))
        def _():
            onward(h, dst, k, 1).start()

    def onward_far(h, dst, k):
        @pl.when(offset == 2)
        def _():
            local(h, dst, k).wait()

    def partner_arrived(h):
        for which in range(2):
            for dz in range(-4, 4):
                at = dz if which == 0 or dz > -4 else 4
                arrived(slot(h, (ylo, 1 - ylo)[which], at, 1 - core), p_recv.at[h, which, (at + 4) % 8])

    low = lane < 64
    zero = jnp.zeros((128, 128), f32)

    def spread(h, dst):
        for b in range(16):
            q_ = flat[h, 32 + b].astype(f32)
            r_ = pltpu.roll(q_, 64, axis=1)
            dst[b, 0:128] = jnp.where(low, q_, zero).astype(bf16)
            dst[b, 128:256] = jnp.where(low, zero, r_).astype(bf16)
            dst[b + 16, 0:128] = jnp.where(low, r_, zero).astype(bf16)
            dst[b + 16, 128:256] = jnp.where(low, zero, q_).astype(bf16)

    def twice(ref, rows=slice(None)):
        v = ref[rows, :]
        return jnp.concatenate([v, v], axis=1)

    def outer_unit(k, d, bp):
        lref, rref, half = ((hl, r1f, 1), (hr, r1m, 0))[d]
        both = lref[pl.ds(pl.multiple_of(k * 128, 128), 128), :]
        lhs0 = jnp.concatenate([both[:, 0:128], both[:, 128:256]], axis=0)
        b0, b1 = 2 * bp, 2 * bp + 1
        rhs0 = jnp.concatenate([flat[half, b0], flat[half, b1]], axis=1)
        o0 = jnp.dot(lhs0, rhs0, preferred_element_type=f32).astype(bf16)
        rhs1 = jnp.concatenate([rref[b0], rref[b1]], axis=1)
        o1 = jnp.dot(both, rhs1, preferred_element_type=f32).astype(bf16)
        for e, b in enumerate((b0, b1)):
            rows = slice(b * 32, b * 32 + 32)
            lanes = slice(e * 128, e * 128 + 128)
            for i in range(8):
                pbuf[rows, i * 128 : i * 128 + 128] = o0[i * 32 : i * 32 + 32, lanes]
            for i in range(4):
                pbuf[rows, (8 + i) * 128 : (9 + i) * 128] = o1[i * 32 : i * 32 + 32, lanes]

    def project_chunk(k, d, n):
        cols = slice(n * 256, n * 256 + 256)
        z_ = jnp.dot((wf, wm)[d][...], pbuf[:, cols], preferred_element_type=f32)
        z_ = jnp.maximum(z_ + twice(bout_b), 0.0)
        zbuf[k, :, cols] = z_ if d == 0 else zbuf[k, :, cols] + z_

    def norm_chunk(k, n):
        pair = zbuf[k, :, n * 256 : n * 256 + 256]
        mean = jnp.mean(pair, axis=0, keepdims=True)
        cen = pair - mean
        var = jnp.mean(cen * cen, axis=0, keepdims=True)
        nbuf[n % 2] = (cen * lax.rsqrt(var + EPSILON) * twice(pg_b) + twice(pb_b)).astype(bf16)

    def up_chunk(n, part):
        rows = slice(part * 128, part * 128 + 128)
        hid = jnp.dot(wup[rows, :], nbuf[n % 2], preferred_element_type=f32)
        hbuf[n % 2, rows, :] = jnp.maximum(hid + twice(bup_b, rows), 0.0).astype(bf16)

    def down_chunk(k, n):
        upd = jnp.dot(wdn[...], hbuf[n % 2], preferred_element_type=f32)
        res = zbuf[k, :, n * 256 : n * 256 + 256] + upd + twice(bdn_b)
        for e in range(2):
            c = 2 * n + e
            t = res[:, e * 128 : e * 128 + 128].T.astype(bf16)
            for q_ in range(4):
                if c < 8:
                    out[c // 4, 4 * k + c % 4, 48 * q_ : 48 * q_ + 32, :] = t[32 * q_ : 32 * q_ + 32]
                else:
                    out[0, 4 * k + c - 8, 48 * q_ + 32 : 48 * q_ + 48, :] = t[16 * q_ : 16 * q_ + 16]
                    out[1, 4 * k + c - 8, 48 * q_ + 32 : 48 * q_ + 48, :] = t[64 + 16 * q_ : 80 + 16 * q_]

    def transition(k):
        stages = []
        for n in range(6):
            stages.append(functools.partial(norm_chunk, k, n))
            for part in range(4):
                stages.append(functools.partial(up_chunk, n, part))
            stages.append(functools.partial(down_chunk, k, n))
        return stages

    partner_arrived(0)

    @pl.when(offset == 0)
    def _():
        make_rows(0, hl)

    partner_arrived(1)

    @pl.when(offset == 0)
    def _():
        onward_root(0, hl, 0)
        make_rows(1, hr)

    spread(1, r1f)
    spread(0, r1m)
    onward_side(0, hl, 0)
    onward_far(0, hl, 0)

    def left_pass(k, carry):
        for bp in range(16):
            outer_unit(k, 0, bp)

        @pl.when(k < 5)
        def _():
            onward_root(0, hl, k + 1)
            onward_side(0, hl, k + 1)
            onward_far(0, hl, k + 1)

        @pl.when(k >= 1)
        def _():
            onward_root(1, hr, k - 1)

        @pl.when(k >= 3)
        def _():
            onward_side(1, hr, k - 3)

        for n in range(6):
            project_chunk(k, 0, n)
        return carry

    lax.fori_loop(0, 6, left_pass, 0)

    onward_far(1, hr, 0)
    for bp in range(16):
        outer_unit(0, 1, bp)
    onward_root(1, hr, 5)
    onward_side(1, hr, 3)
    for n in range(6):
        project_chunk(0, 1, n)

    def right_pass(k, carry):
        onward_far(1, hr, k)
        stages = transition(k - 1)
        done = 0
        for bp in range(16):
            outer_unit(k, 1, bp)
            while done < (bp + 1) * len(stages) // 16:
                stages[done]()
                done += 1

        @pl.when(k < 3)
        def _():
            onward_side(1, hr, k + 3)

        for n in range(6):
            project_chunk(k, 1, n)
        return carry

    lax.fori_loop(1, 6, right_pass, 0)
    for stage_ in transition(5):
        stage_()

    for h, dst in ((0, hl), (1, hr)):
        for k in range(6):

            @pl.when(far_source)
            def _(h=h, dst=dst, k=k):
                first(h, dst, k).wait_send()

            @pl.when(offset == 0)
            def _(h=h, dst=dst, k=k):
                onward(h, dst, k, 0).wait_send()
                onward(h, dst, k, 1).wait_send()

            @pl.when(offset == (1, 3)[k % 2])
            def _(h=h, dst=dst, k=k):
                onward(h, dst, k, k % 2).wait_send()

    for c in sent:
        c.wait_send()


def fused(x, *params):
    rows = x.shape[0]
    bf16, f32 = jnp.bfloat16, jnp.float32
    vmem = pl.BlockSpec(memory_space=pltpu.VMEM)
    dma = pltpu.SemaphoreType.DMA
    args = (x,) + tuple(p[None, :] if p.ndim == 1 else p for p in params)
    out = pl.pallas_call(
        fused_kernel,
        in_specs=[vmem] * len(args),
        out_specs=vmem,
        out_shape=jax.ShapeDtypeStruct((2, 24, 192, 128), bf16),
        scratch_shapes=[
            pltpu.VMEM((2, 48, 32, rows, 128), bf16),
            pltpu.VMEM((768, 256), bf16),
            pltpu.VMEM((768, 256), bf16),
            pltpu.VMEM((2, 48, rows, 128), f32),
            pltpu.VMEM((2, 48, rows, 128), bf16),
            pltpu.VMEM((2, 768, 128), f32),
            pltpu.VMEM((2, 768, 256), bf16),
            pltpu.VMEM((32, 256, 128), bf16),
            pltpu.VMEM((32, 256, 128), bf16),
            pltpu.VMEM((1024, 1536), bf16),
            pltpu.VMEM((6, 128, 1536), f32),
            pltpu.VMEM((2, 128, 256), bf16),
            pltpu.VMEM((2, 512, 256), bf16),
            pltpu.VMEM((1024, 128), f32),
            pltpu.VMEM((128, 1024), bf16),
            pltpu.VMEM((128, 1024), bf16),
            pltpu.VMEM((512, 128), bf16),
            pltpu.VMEM((128, 512), bf16),
            pltpu.VMEM((128, 128), f32),
            pltpu.VMEM((128, 128), f32),
            pltpu.VMEM((128, 128), f32),
            pltpu.VMEM((128, 128), f32),
            pltpu.VMEM((512, 128), f32),
            dma((2,)),
            dma((2, 2, 4)),
            dma((2, 2, 4)),
            dma((2, 4)),
            dma((2, 4)),
            dma((2, 8)),
            dma((2, 8)),
            dma((2, 2, 8)),
            dma((2, 2, 8)),
            dma((2, 6)),
            dma((2, 2, 6)),
            dma((2, 6)),
        ],
        compiler_params=pltpu.CompilerParams(
            collective_id=0, has_side_effects=True, vmem_limit_bytes=48 * 1024 * 1024
        ),
        name="fused",
    )(*args)
    return out.reshape(48, 192, 128)


def shards(
    alignment,
    alignment_norm_gain,
    alignment_norm_bias,
    projection_weight,
    projection_bias_pair,
    *rest,
):
    return fused(
        alignment,
        alignment_norm_gain,
        alignment_norm_bias,
        projection_weight.T,
        projection_bias_pair,
        *rest,
    )


def solution(mesh):
    return jax.shard_map(
        shards,
        mesh=mesh,
        in_specs=(P("row", "col", None),) + (P(),) * 12,
        out_specs=P("row", "col", None),
        check_vma=False,
    )
```

```python
import functools

import jax
import jax.numpy as jnp
from jax import lax
from jax.experimental import pallas as pl
from jax.experimental.pallas import tpu as pltpu
from jax.sharding import PartitionSpec as P

EPSILON = 1e-05
VMEM_LIMIT = 60 * 1024 * 1024


MESH = pl.DeviceIdType.MESH
ZN, XN = 8, 4


def project_block(x_ref, gain_ref, bias_ref, w_ref, pbias_ref, stage):
    rows = x_ref.shape[0]
    low = lax.broadcasted_iota(jnp.int32, (1, 128), 1) < 64
    w2 = jnp.concatenate([w_ref[...], w_ref[...]], axis=0)
    pbias = jnp.concatenate([pbias_ref[...], pbias_ref[...]], axis=1)
    for s in range(rows):
        x = x_ref[s].astype(jnp.float32)
        mean = jnp.mean(x, axis=-1, keepdims=True)
        cen = x - mean
        var = jnp.mean(cen * cen, axis=-1, keepdims=True)
        normed = (cen * lax.rsqrt(var + EPSILON) * gain_ref[...] + bias_ref[...]).astype(jnp.bfloat16)
        d = lax.dot_general(normed, w2, (((1,), (1,)), ((), ())), preferred_element_type=jnp.float32)
        d = d + pbias
        t0 = jnp.concatenate([d[48 * q : 48 * q + 32] for q in range(4)], axis=0).T
        t1 = jnp.concatenate([d[48 * q + 32 : 48 * q + 48] for q in range(4)] * 2, axis=0).T
        for h in range(2):
            stage[h, 0:32, s, :] = t0[32 * h : 32 * h + 32]
            stage[h, 32:48, s, :] = jnp.where(low, t1[32 * h : 32 * h + 16], t1[32 * h + 16 : 32 * h + 32])


def fused_kernel(
    *refs,
):
    ins, vins = refs[:13], refs[14:27]
    out = refs[13]
    in_sem = refs[27]
    fetch = [pltpu.make_async_copy(a, v, in_sem.at[i]) for i, (a, v) in enumerate(zip(ins, vins))]
    for c in fetch:
        c.start()
    fused_body(fetch, *vins, out, *refs[28:])


def fused_body(
    fetch, x_ref, gain_ref, bias_ref, w_ref, pbias_ref, w_out, bout, pg, pb, w_up, bup, w_down, bdn, out,
    obuf, o_sem, g, hl, hr, stage, block, hstage, hsend, r1f, r1m, pbuf, zbuf, nbuf, hbuf, wtmp,
    wf, wm, wup, wdn, bout_b, pg_b, pb_b, bdn_b, bup_b,
    own_sem, l_send, l_recv, r_send, r_recv, y_send, y_recv, p_send, p_recv, hs_sem, hf_sem, h_recv,
):
    bf16, f32 = jnp.bfloat16, jnp.float32

    def prepare_weights():
        total = 4 * 32
        wtmp[...] = w_out[...].astype(f32) * (1.0 / total)
        for m in range(8):
            rows = slice(m * 128, m * 128 + 128)
            wm[:, rows] = wtmp[rows, :].T.astype(bf16)
            picked = [wtmp[pl.ds(4 * m + e, 32, stride=32), :] for e in range(4)]
            wf[:, rows] = jnp.concatenate(picked, axis=0).T.astype(bf16)
        for m in range(4):
            rows = slice(m * 128, m * 128 + 128)
            wup[rows, :] = w_up[:, rows].astype(f32).T.astype(bf16)
            wdn[:, rows] = w_down[rows, :].astype(f32).T.astype(bf16)
            bup_b[rows, :] = jnp.broadcast_to(bup[:, rows], (128, 128)).T
        for wide, narrow in ((bout_b, bout), (pg_b, pg), (pb_b, pb), (bdn_b, bdn)):
            wide[...] = jnp.broadcast_to(narrow[...], (128, 128)).T

    row, col = lax.axis_index("row"), lax.axis_index("col")
    core = lax.rem(row, 2)
    z = lax.rem(row // 2, ZN)
    ylo = row // (2 * ZN)
    x = lax.rem(col, XN)
    yhi = col // XN

    def row_of(ylo_, z_, core_):
        return (ylo_ * ZN + z_) * 2 + core_

    zup, zdn = lax.rem(z + 1, ZN), lax.rem(z + ZN - 1, ZN)
    up = (row_of(ylo, zup, core), col)
    down = (row_of(ylo, zdn, core), col)
    across = (row_of(1 - ylo, z, core), col)
    partner = (row_of(ylo, z, 1 - core), col)
    xup = (row, yhi * XN + lax.rem(x + 1, XN))
    xdn = (row, yhi * XN + lax.rem(x + XN - 1, XN))
    facing = (row_of(1 - ylo, z, core), (1 - yhi) * XN + x)

    barrier = pltpu.get_barrier_semaphore()
    far = (row, yhi * XN + lax.rem(x + 2, XN))
    diagonal = [(facing[0], (1 - yhi) * XN + lax.rem(x + d, XN)) for d in range(1, XN)]
    others = (up, down, across, partner, xup, xdn, far, facing, *diagonal)
    for dev in others:
        pl.semaphore_signal(barrier, inc=1, device_id=dev, device_id_type=MESH)

    for c in fetch[:5]:
        c.wait()
    project_block(x_ref, gain_ref, bias_ref, w_ref, pbias_ref, stage)
    block[...] = stage[...].astype(bf16)
    own = [pltpu.make_async_copy(block.at[h], g.at[h, :, row], own_sem.at[h]) for h in range(2)]
    for c in own:
        c.start()
    pl.semaphore_wait(barrier, len(others))

    sent = []

    def slot(h, ylo_, dz, core_):
        return g.at[h, :, row_of(ylo_, lax.rem(z + dz + ZN, ZN), core_)]

    def copy(ref, send, recv, dev):
        c = pltpu.make_async_remote_copy(ref, ref, send, recv, device_id=dev, device_id_type=MESH)
        return c

    def send(ref, s, r, dev):
        c = copy(ref, s, r, dev)
        c.start()
        sent.append(c)

    def arrived(ref, r):
        copy(ref, own_sem.at[0], r, partner).wait_recv()

    def ring_l(which, ylo_, dz):
        top, bottom = (4, 3) if which == 0 else (3, 4)
        ref = slot(0, ylo_, dz, core)
        if dz <= 0 and -dz < top:
            t = -dz
            send(ref, l_send.at[which, 0, t], l_recv.at[which, 0, t], up)
        if dz >= 0 and dz < bottom:
            t = dz
            send(ref, l_send.at[which, 1, t], l_recv.at[which, 1, t], down)

    def ring_r(dz):
        ref = slot(1, ylo, dz, core)
        if dz <= 0 and -dz < 4:
            send(ref, r_send.at[0, -dz], r_recv.at[0, -dz], up)
        if dz >= 0 and dz < 3:
            send(ref, r_send.at[1, dz], r_recv.at[1, dz], down)
        send(ref, y_send.at[1, dz + 4], y_recv.at[1, dz + 4], across)

    def pslot(h, which, ylo_, dz):
        i = (dz + 4) % 8
        send(slot(h, ylo_, dz, core), p_send.at[h, which, i], p_recv.at[h, which, i], partner)

    own[0].wait()
    own[1].wait()
    ring_l(0, ylo, 0)
    send(slot(0, ylo, 0, core), y_send.at[0, 0], y_recv.at[0, 0], across)
    ring_r(0)
    pslot(0, 0, ylo, 0)
    pslot(1, 0, ylo, 0)
    for c in fetch[5:]:
        c.wait()
    prepare_weights()
    arrived(slot(0, 1 - ylo, 0, core), y_recv.at[0, 0])
    ring_l(1, 1 - ylo, 0)
    pslot(0, 1, 1 - ylo, 0)
    prev = [0]
    for t in range(1, 5):
        for dz in (-t, t):
            if dz == 4:
                continue
            way = 0 if dz < 0 else 1
            arrived(slot(0, ylo, dz, core), l_recv.at[0, way, t - 1])
            ring_l(0, ylo, dz)
            arrived(slot(1, ylo, dz, core), r_recv.at[way, t - 1])
            ring_r(dz)
            pslot(0, 0, ylo, dz)
            pslot(1, 0, ylo, dz)
        for dz in (-t, t):
            if dz == -4:
                continue
            way = 0 if dz < 0 else 1
            arrived(slot(0, 1 - ylo, dz, core), l_recv.at[1, way, t - 1])
            ring_l(1, 1 - ylo, dz)
            pslot(0, 1, 1 - ylo, dz)
        for dz in prev:
            arrived(slot(1, 1 - ylo, dz, core), y_recv.at[1, dz + 4])
            pslot(1, 1, 1 - ylo, dz)
        prev = [dz for dz in (-t, t) if dz != 4]
    for dz in prev:
        arrived(slot(1, 1 - ylo, dz, core), y_recv.at[1, dz + 4])
        pslot(1, 1, 1 - ylo, dz)

    offset = lax.rem(x - z // 2 + XN, XN)
    q = lax.rem(row, 4)
    shift0 = lax.rem(128 - 32 * q, 128)
    shift1 = lax.rem(128 - 32 * q + 64, 128)
    shift2 = lax.rem(128 - 16 * q + 32, 128)
    lane = lax.broadcasted_iota(jnp.int32, (1, 128), 1)
    flat = g.reshape(2, 48, 128, 128)
    self_source = (offset == 0) & (ylo == yhi)
    far_source = (offset == 0) & (ylo != yhi)

    def chunk(ref, k):
        return ref.at[pl.ds(pl.multiple_of(k * 128, 128), 128)]

    def local(h, dst, k):
        return pltpu.make_async_copy(chunk(hsend.at[h], k), chunk(dst, k), h_recv.at[h, k])

    def first(h, dst, k):
        return pltpu.make_async_remote_copy(
            chunk(hsend.at[h], k), chunk(dst, k), hs_sem.at[h, k], h_recv.at[h, k], device_id=facing, device_id_type=MESH
        )

    def direct(h, dst, k, way):
        step_ = (1, XN - 1, 2)[way]
        dev = (jnp.where(ylo == yhi, row, facing[0]), jnp.where(ylo == yhi, yhi, 1 - yhi) * XN + lax.rem(x + step_, XN))
        return pltpu.make_async_remote_copy(
            chunk(hsend.at[h], k), chunk(dst, k), hf_sem.at[h, way, k], h_recv.at[h, k], device_id=dev, device_id_type=MESH
        )

    def onward(h, dst, k, way):
        return copy(chunk(dst, k), hf_sem.at[h, way, k], h_recv.at[h, k], (xup, xdn)[way])

    def make_rows(h, dst):
        for p in range(16):
            a0 = pltpu.roll(flat[h, p].astype(f32), shift0, axis=1)
            a1 = pltpu.roll(flat[h, p + 16].astype(f32), shift1, axis=1)
            b = pltpu.roll(flat[h, 32 + p].astype(f32), shift2, axis=1)
            t = jnp.where(lane < 32, a0, jnp.where((lane >= 64) & (lane < 96), a1, b)).T
            for e in range(2):
                at = pl.ds(p + 16 * e, 24, stride=32)
                hstage[0, at, :] = t[64 * e : 64 * e + 24]
                hstage[1, at, :] = t[64 * e + 24 : 64 * e + 48]
        hsend[h, :, 0:128] = hstage[0].astype(bf16)
        hsend[h, :, 128:256] = hstage[1].astype(bf16)

        @pl.when(ylo == yhi)
        def _():
            for k in range(6):
                local(h, dst, k).start()
                direct(h, dst, k, 0).start()
                direct(h, dst, k, 1).start()
                if k == 0:
                    direct(h, dst, k, 2).start()

        @pl.when(ylo != yhi)
        def _():
            for k in range(6):
                first(h, dst, k).start()
                if k == 0:
                    for way in range(3):
                        direct(h, dst, k, way).start()

    def pass_root(h, dst, k):
        @pl.when(offset == 0)
        def _():
            local(h, dst, k).wait()

        @pl.when(far_source & (k > 0))
        def _():
            onward(h, dst, k, 0).start()
            onward(h, dst, k, 1).start()

    def pass_side(h, dst, k):
        @pl.when((offset == 1) | (offset == 3))
        def _():
            local(h, dst, k).wait()

        @pl.when((offset == 1) & (lax.rem(k, 2) == 0) & (k > 0))
        def _():
            onward(h, dst, k, 0).start()

        @pl.when((offset == 3) & (lax.rem(k, 2) == 1))
        def _():
            onward(h, dst, k, 1).start()

    def pass_far(h, dst, k):
        @pl.when(offset == 2)
        def _():
            local(h, dst, k).wait()

    def partner_arrived(h):
        for which in range(2):
            for dz in range(-4, 4):
                at = dz if which == 0 or dz > -4 else 4
                arrived(slot(h, (ylo, 1 - ylo)[which], at, 1 - core), p_recv.at[h, which, (at + 4) % 8])

    low = lane < 64
    zero = jnp.zeros((128, 128), f32)

    def spread(h, dst):
        for b in range(16):
            q_ = flat[h, 32 + b].astype(f32)
            r_ = pltpu.roll(q_, 64, axis=1)
            dst[b, 0:128] = jnp.where(low, q_, zero).astype(bf16)
            dst[b, 128:256] = jnp.where(low, zero, r_).astype(bf16)
            dst[b + 16, 0:128] = jnp.where(low, r_, zero).astype(bf16)
            dst[b + 16, 128:256] = jnp.where(low, zero, q_).astype(bf16)

    def twice(ref, rows=slice(None)):
        v = ref[rows, :]
        return jnp.concatenate([v, v], axis=1)

    def outer_unit(k, d, slot_, bp):
        lref, rref, half = ((hl, r1f, 1), (hr, r1m, 0))[d]
        both = lref[pl.ds(pl.multiple_of(k * 128, 128), 128), :]
        lhs0 = jnp.concatenate([both[:, 0:128], both[:, 128:256]], axis=0)
        b0, b1 = 2 * bp, 2 * bp + 1
        rhs0 = jnp.concatenate([flat[half, b0], flat[half, b1]], axis=1)
        o0 = jnp.dot(lhs0, rhs0, preferred_element_type=f32).astype(bf16)
        rhs1 = jnp.concatenate([rref[b0], rref[b1]], axis=1)
        o1 = jnp.dot(both, rhs1, preferred_element_type=f32).astype(bf16)
        for e, b in enumerate((b0, b1)):
            rows = slice(b * 32, b * 32 + 32)
            lanes = slice(e * 128, e * 128 + 128)
            for i in range(8):
                pbuf[slot_, rows, i * 128 : i * 128 + 128] = o0[i * 32 : i * 32 + 32, lanes]
            for i in range(4):
                pbuf[slot_, rows, (8 + i) * 128 : (9 + i) * 128] = o1[i * 32 : i * 32 + 32, lanes]

    def project_chunk(k, d, slot_, n):
        cols = slice(n * 256, n * 256 + 256)
        z_ = jnp.dot((wf, wm)[d][...], pbuf[slot_, :, cols], preferred_element_type=f32)
        z_ = jnp.maximum(z_ + twice(bout_b), 0.0)
        zbuf[k, :, cols] = z_ if d == 0 else zbuf[k, :, cols] + z_

    def norm_chunk(k, n):
        pair = zbuf[k, :, n * 256 : n * 256 + 256]
        mean = jnp.mean(pair, axis=0, keepdims=True)
        cen = pair - mean
        var = jnp.mean(cen * cen, axis=0, keepdims=True)
        nbuf[n % 2] = (cen * lax.rsqrt(var + EPSILON) * twice(pg_b) + twice(pb_b)).astype(bf16)

    def up_chunk(n, part):
        rows = slice(part * 128, part * 128 + 128)
        hid = jnp.dot(wup[rows, :], nbuf[n % 2], preferred_element_type=f32)
        hbuf[n % 2, rows, :] = jnp.maximum(hid + twice(bup_b, rows), 0.0).astype(bf16)

    def down_chunk(k, n):
        upd = jnp.dot(wdn[...], hbuf[n % 2], preferred_element_type=f32)
        res = zbuf[k, :, n * 256 : n * 256 + 256] + upd + twice(bdn_b)
        for e in range(2):
            c = 2 * n + e
            t = res[:, e * 128 : e * 128 + 128].T.astype(bf16)
            for q_ in range(4):
                if c < 8:
                    obuf[c // 4, 4 * k + c % 4, 48 * q_ : 48 * q_ + 32, :] = t[32 * q_ : 32 * q_ + 32]
                else:
                    obuf[0, 4 * k + c - 8, 48 * q_ + 32 : 48 * q_ + 48, :] = t[16 * q_ : 16 * q_ + 16]
                    obuf[1, 4 * k + c - 8, 48 * q_ + 32 : 48 * q_ + 48, :] = t[64 + 16 * q_ : 80 + 16 * q_]

    def outer(k, d, slot_):
        return [functools.partial(outer_unit, k, d, slot_, bp) for bp in range(16)]

    def project(k, d, slot_):
        return [functools.partial(project_chunk, k, d, slot_, n) for n in range(6)]

    def transition(k):
        stages = []
        for n in range(0, 6, 2):
            both = (n, n + 1)
            stages += [functools.partial(norm_chunk, k, m) for m in both]
            for part in range(4):
                stages += [functools.partial(up_chunk, m, part) for m in both]
            stages += [functools.partial(down_chunk, k, m) for m in both]
        return stages

    def interleave(*lists):
        steps = [((i + 0.5) / len(l), j, f) for j, l in enumerate(lists) for i, f in enumerate(l)]
        for _, _, f in sorted(steps, key=lambda t: t[:2]):
            f()

    partner_arrived(0)

    @pl.when(offset == 0)
    def _():
        make_rows(0, hl)

    partner_arrived(1)
    spread(1, r1f)

    @pl.when(offset == 0)
    def _():
        make_rows(1, hr)

    spread(0, r1m)

    def pass_left(k):
        pass_root(0, hl, k)
        pass_side(0, hl, k)
        pass_far(0, hl, k)

    pass_left(0)
    interleave(outer(0, 0, 0))

    def left_step(k, parity):
        pass_left(k + 1)

        @pl.when(k >= 1)
        def _():
            pass_root(1, hr, k - 1)

        @pl.when(k >= 3)
        def _():
            pass_side(1, hr, k - 3)

        interleave(outer(k + 1, 0, 1 - parity), project(k, 0, parity))

    def left_pair(t, carry):
        left_step(2 * t, 0)
        left_step(2 * t + 1, 1)
        return carry

    lax.fori_loop(0, 2, left_pair, 0)
    left_step(jnp.int32(4), 0)

    pass_root(1, hr, 4)
    pass_root(1, hr, 5)
    pass_side(1, hr, 2)
    pass_far(1, hr, 0)
    interleave(outer(0, 1, 0), project(5, 0, 1))
    pass_side(1, hr, 3)
    pass_far(1, hr, 1)
    interleave(outer(1, 1, 1), project(0, 1, 0))

    def results(k):
        return [
            pltpu.make_async_copy(obuf.at[w, pl.ds(4 * k, 4)], out.at[w, pl.ds(4 * k, 4)], o_sem.at[w, k])
            for w in range(2)
        ]

    def right_step(k, parity):
        @pl.when(k < 3)
        def _():
            pass_side(1, hr, k + 3)

        pass_far(1, hr, k + 1)
        interleave(outer(k + 1, 1, 1 - parity), project(k, 1, parity), transition(k - 1))
        for c in results(k - 1):
            c.start()

    def right_pair(t, carry):
        right_step(2 * t + 1, 1)
        right_step(2 * t + 2, 0)
        return carry

    lax.fori_loop(0, 2, right_pair, 0)
    interleave(project(5, 1, 1), transition(4))
    for c in results(4):
        c.start()
    interleave(transition(5))
    for c in results(5):
        c.start()

    for h, dst in ((0, hl), (1, hr)):
        for k in range(6):

            @pl.when(far_source)
            def _(h=h, dst=dst, k=k):
                first(h, dst, k).wait_send()

            @pl.when(offset == 0)
            def _(h=h, dst=dst, k=k):
                for way in range(3 if k == 0 else 2):
                    direct(h, dst, k, way).wait_send()

            if k > 0:

                @pl.when(offset == (1, 3)[k % 2])
                def _(h=h, dst=dst, k=k):
                    onward(h, dst, k, k % 2).wait_send()

    for c in sent:
        c.wait_send()
    for k in range(6):
        for c in results(k):
            c.wait()


def fused(x, *params):
    rows = x.shape[0]
    bf16, f32 = jnp.bfloat16, jnp.float32
    dma = pltpu.SemaphoreType.DMA
    args = (x,) + tuple(p[None, :] if p.ndim == 1 else p for p in params)
    out = pl.pallas_call(
        fused_kernel,
        in_specs=[pl.BlockSpec(memory_space=pltpu.HBM)] * len(args),
        out_specs=pl.BlockSpec(memory_space=pltpu.HBM),
        out_shape=jax.ShapeDtypeStruct((2, 24, 192, 128), bf16),
        scratch_shapes=[pltpu.VMEM(a.shape, a.dtype) for a in args] + [
            dma((len(args),)),
            pltpu.VMEM((2, 24, 192, 128), bf16),
            dma((2, 6)),
            pltpu.VMEM((2, 48, 32, rows, 128), bf16),
            pltpu.VMEM((768, 256), bf16),
            pltpu.VMEM((768, 256), bf16),
            pltpu.VMEM((2, 48, rows, 128), f32),
            pltpu.VMEM((2, 48, rows, 128), bf16),
            pltpu.VMEM((2, 768, 128), f32),
            pltpu.VMEM((2, 768, 256), bf16),
            pltpu.VMEM((32, 256, 128), bf16),
            pltpu.VMEM((32, 256, 128), bf16),
            pltpu.VMEM((2, 1024, 1536), bf16),
            pltpu.VMEM((6, 128, 1536), f32),
            pltpu.VMEM((2, 128, 256), bf16),
            pltpu.VMEM((2, 512, 256), bf16),
            pltpu.VMEM((1024, 128), f32),
            pltpu.VMEM((128, 1024), bf16),
            pltpu.VMEM((128, 1024), bf16),
            pltpu.VMEM((512, 128), bf16),
            pltpu.VMEM((128, 512), bf16),
            pltpu.VMEM((128, 128), f32),
            pltpu.VMEM((128, 128), f32),
            pltpu.VMEM((128, 128), f32),
            pltpu.VMEM((128, 128), f32),
            pltpu.VMEM((512, 128), f32),
            dma((2,)),
            dma((2, 2, 4)),
            dma((2, 2, 4)),
            dma((2, 4)),
            dma((2, 4)),
            dma((2, 8)),
            dma((2, 8)),
            dma((2, 2, 8)),
            dma((2, 2, 8)),
            dma((2, 6)),
            dma((2, 3, 6)),
            dma((2, 6)),
        ],
        compiler_params=pltpu.CompilerParams(
            collective_id=0, has_side_effects=True, vmem_limit_bytes=67043328
        ),
        name="fused",
    )(*args)
    return out.reshape(48, 192, 128)


def shards(
    alignment,
    alignment_norm_gain,
    alignment_norm_bias,
    projection_weight,
    projection_bias_pair,
    *rest,
):
    return fused(
        alignment,
        alignment_norm_gain,
        alignment_norm_bias,
        projection_weight.T,
        projection_bias_pair,
        *rest,
    )


def solution(mesh):
    return jax.shard_map(
        shards,
        mesh=mesh,
        in_specs=(P("row", "col", None),) + (P(),) * 12,
        out_specs=P("row", "col", None),
        check_vma=False,
    )
```

```python
import functools

import jax
import jax.numpy as jnp
from jax import lax
from jax.experimental import pallas as pl
from jax.experimental.pallas import tpu as pltpu
from jax.sharding import PartitionSpec as P

EPSILON = 1e-05
VMEM_LIMIT = 60 * 1024 * 1024


MESH = pl.DeviceIdType.MESH
ZN, XN = 8, 4


def project_block(x_ref, gain_ref, bias_ref, w_ref, pbias_ref, stage):
    rows = x_ref.shape[0]
    low = lax.broadcasted_iota(jnp.int32, (1, 128), 1) < 64
    w2 = jnp.concatenate([w_ref[...], w_ref[...]], axis=0)
    pbias = jnp.concatenate([pbias_ref[...], pbias_ref[...]], axis=1)
    for s in range(rows):
        x = x_ref[s].astype(jnp.float32)
        mean = jnp.mean(x, axis=-1, keepdims=True)
        cen = x - mean
        var = jnp.mean(cen * cen, axis=-1, keepdims=True)
        normed = (cen * lax.rsqrt(var + EPSILON) * gain_ref[...] + bias_ref[...]).astype(jnp.bfloat16)
        d = lax.dot_general(normed, w2, (((1,), (1,)), ((), ())), preferred_element_type=jnp.float32)
        d = d + pbias
        t0 = jnp.concatenate([d[48 * q : 48 * q + 32] for q in range(4)], axis=0).T
        t1 = jnp.concatenate([d[48 * q + 32 : 48 * q + 48] for q in range(4)] * 2, axis=0).T
        for h in range(2):
            stage[h, 0:32, s, :] = t0[32 * h : 32 * h + 32]
            stage[h, 32:48, s, :] = jnp.where(low, t1[32 * h : 32 * h + 16], t1[32 * h + 16 : 32 * h + 32])


def fused_kernel(
    *refs,
):
    ins, vins = refs[:13], refs[14:27]
    out = refs[13]
    in_sem = refs[27]
    fetch = [pltpu.make_async_copy(a, v, in_sem.at[i]) for i, (a, v) in enumerate(zip(ins, vins))]
    for c in fetch:
        c.start()
    fused_body(fetch, *vins, out, *refs[28:])


def fused_body(
    fetch, x_ref, gain_ref, bias_ref, w_ref, pbias_ref, w_out, bout, pg, pb, w_up, bup, w_down, bdn, out,
    g, hl, hr, stage, block, hstage, hsend, r1f, r1m, pbuf, zbuf, nbuf, hbuf, wtmp,
    wf, wm, wup, wdn, bout_b, pg_b, pb_b, bdn_b, bup_b,
    own_sem, z_send, z_recv, y_send, y_recv, p_send, p_recv, hs_sem, hf_sem, h_recv,
):
    bf16, f32 = jnp.bfloat16, jnp.float32

    def prepare_weights():
        total = 4 * 32
        wtmp[...] = w_out[...].astype(f32) * (1.0 / total)
        for m in range(8):
            rows = slice(m * 128, m * 128 + 128)
            wm[:, rows] = wtmp[rows, :].T.astype(bf16)
            picked = [wtmp[pl.ds(4 * m + e, 32, stride=32), :] for e in range(4)]
            wf[:, rows] = jnp.concatenate(picked, axis=0).T.astype(bf16)
        for m in range(4):
            rows = slice(m * 128, m * 128 + 128)
            wup[rows, :] = w_up[:, rows].astype(f32).T.astype(bf16)
            wdn[:, rows] = w_down[rows, :].astype(f32).T.astype(bf16)
            bup_b[rows, :] = jnp.broadcast_to(bup[:, rows], (128, 128)).T
        for wide, narrow in ((bout_b, bout), (pg_b, pg), (pb_b, pb), (bdn_b, bdn)):
            wide[...] = jnp.broadcast_to(narrow[...], (128, 128)).T

    row, col = lax.axis_index("row"), lax.axis_index("col")
    core = lax.rem(row, 2)
    z = lax.rem(row // 2, ZN)
    ylo = row // (2 * ZN)
    x = lax.rem(col, XN)
    yhi = col // XN

    def row_of(ylo_, z_, core_):
        return (ylo_ * ZN + z_) * 2 + core_

    zup, zdn = lax.rem(z + 1, ZN), lax.rem(z + ZN - 1, ZN)
    up = (row_of(ylo, zup, core), col)
    down = (row_of(ylo, zdn, core), col)
    across = (row_of(1 - ylo, z, core), col)
    partner = (row_of(ylo, z, 1 - core), col)
    xup = (row, yhi * XN + lax.rem(x + 1, XN))
    xdn = (row, yhi * XN + lax.rem(x + XN - 1, XN))
    facing = (row_of(1 - ylo, z, core), (1 - yhi) * XN + x)

    barrier = pltpu.get_barrier_semaphore()
    far = (row, yhi * XN + lax.rem(x + 2, XN))
    diagonal = [(facing[0], (1 - yhi) * XN + lax.rem(x + d, XN)) for d in range(1, XN)]
    near2 = [(row_of(ylo, lax.rem(z + d, ZN), core), col) for d in (2, ZN - 2)]
    others = (up, down, *near2, across, partner, xup, xdn, far, facing, *diagonal)
    for dev in others:
        pl.semaphore_signal(barrier, inc=1, device_id=dev, device_id_type=MESH)

    for c in fetch[:5]:
        c.wait()
    project_block(x_ref, gain_ref, bias_ref, w_ref, pbias_ref, stage)
    block[...] = stage[...].astype(bf16)
    own = [pltpu.make_async_copy(block.at[h], g.at[h, :, row], own_sem.at[h]) for h in range(2)]
    for c in own:
        c.start()
    pl.semaphore_wait(barrier, len(others))

    sent = []

    def slot(h, ylo_, dz, core_):
        return g.at[h, :, row_of(ylo_, lax.rem(z + dz + ZN, ZN), core_)]

    def copy(ref, send, recv, dev):
        c = pltpu.make_async_remote_copy(ref, ref, send, recv, device_id=dev, device_id_type=MESH)
        return c

    def send(ref, s, r, dev):
        c = copy(ref, s, r, dev)
        c.start()
        sent.append(c)

    def arrived(ref, r):
        copy(ref, own_sem.at[0], r, partner).wait_recv()

    up2 = (row_of(ylo, lax.rem(z + 2, ZN), core), col)
    down2 = (row_of(ylo, lax.rem(z + ZN - 2, ZN), core), col)

    def along(h, dz, there, dev):
        send(slot(h, ylo, dz, core), z_send.at[h, there + 4], z_recv.at[h, there + 4], dev)

    def got(h, dz):
        arrived(slot(h, ylo, dz, core), z_recv.at[h, dz + 4])

    def over(h, dz):
        send(slot(h, ylo, dz, core), y_send.at[h, dz + 4], y_recv.at[h, dz + 4], across)

    def got_over(h, dz):
        arrived(slot(h, 1 - ylo, dz, core), y_recv.at[h, dz + 4])

    def share(h, ylo_, dz):
        copy(slot(h, ylo_, dz, core), p_send.at[h], p_recv.at[h], partner).start()

    def shared(h):
        whole = g.at[h, 0:24]
        return copy(whole, p_send.at[h], p_recv.at[h], partner)

    own[0].wait()
    along(0, 0, -1, up)
    along(0, 0, 1, down)
    along(0, 0, -2, up2)
    along(0, 0, 2, down2)
    over(0, 0)
    share(0, ylo, 0)
    own[1].wait()
    along(1, 0, -1, up)
    along(1, 0, 1, down)
    share(1, ylo, 0)
    for c in fetch[5:]:
        c.wait()
    prepare_weights()
    for dz in (-1, 1):
        got(0, dz)
        over(0, dz)
        share(0, ylo, dz)
    got(0, -2)
    along(0, -2, -3, up)
    along(0, -2, -4, up2)
    over(0, -2)
    share(0, ylo, -2)
    got(0, 2)
    along(0, 2, 3, down)
    over(0, 2)
    share(0, ylo, 2)
    for dz in (-1, 1):
        got(1, dz)
        along(1, dz, dz * 2, up if dz < 0 else down)
        share(1, ylo, dz)
    for dz in (-3, 3, -4):
        got(0, dz)
        over(0, dz)
        share(0, ylo, dz)
    for dz in (-2, 2):
        got(1, dz)
        along(1, dz, dz * 3 // 2, up if dz < 0 else down)
        share(1, ylo, dz)
    for dz in (0, -1, 1, -2, 2):
        got_over(0, dz)
        share(0, 1 - ylo, dz)
    got(1, -3)
    along(1, -3, -4, up)
    share(1, ylo, -3)
    for dz in (-3, 3, -4):
        got_over(0, dz)
        share(0, 1 - ylo, dz)
    for dz in (0, -1, 1, -2, 2, -3):
        over(1, dz)
    got(1, 3)
    over(1, 3)
    share(1, ylo, 3)
    got(1, -4)
    over(1, -4)
    share(1, ylo, -4)

    offset = lax.rem(x - z // 2 + XN, XN)
    q = lax.rem(row, 4)
    shift0 = lax.rem(128 - 32 * q, 128)
    shift1 = lax.rem(128 - 32 * q + 64, 128)
    shift2 = lax.rem(128 - 16 * q + 32, 128)
    lane = lax.broadcasted_iota(jnp.int32, (1, 128), 1)
    flat = g.reshape(2, 48, 128, 128)
    self_source = (offset == 0) & (ylo == yhi)
    far_source = (offset == 0) & (ylo != yhi)

    def chunk(ref, k):
        return ref.at[pl.ds(pl.multiple_of(k * 128, 128), 128)]

    def local(h, dst, k):
        return pltpu.make_async_copy(chunk(hsend.at[h], k), chunk(dst, k), h_recv.at[h, k])

    def first(h, dst, k):
        return pltpu.make_async_remote_copy(
            chunk(hsend.at[h], k), chunk(dst, k), hs_sem.at[h, k], h_recv.at[h, k], device_id=facing, device_id_type=MESH
        )

    def direct(h, dst, k, way):
        step_ = (1, XN - 1, 2)[way]
        dev = (jnp.where(ylo == yhi, row, facing[0]), jnp.where(ylo == yhi, yhi, 1 - yhi) * XN + lax.rem(x + step_, XN))
        return pltpu.make_async_remote_copy(
            chunk(hsend.at[h], k), chunk(dst, k), hf_sem.at[h, way, k], h_recv.at[h, k], device_id=dev, device_id_type=MESH
        )

    def onward(h, dst, k, way):
        return copy(chunk(dst, k), hf_sem.at[h, way, k], h_recv.at[h, k], (xup, xdn)[way])

    def make_rows(h):
        for p in range(16):
            a0 = pltpu.roll(flat[h, p].astype(f32), shift0, axis=1)
            a1 = pltpu.roll(flat[h, p + 16].astype(f32), shift1, axis=1)
            b = pltpu.roll(flat[h, 32 + p].astype(f32), shift2, axis=1)
            t = jnp.where(lane < 32, a0, jnp.where((lane >= 64) & (lane < 96), a1, b)).T
            for e in range(2):
                at = pl.ds(p + 16 * e, 24, stride=32)
                hstage[0, at, :] = t[64 * e : 64 * e + 24]
                hstage[1, at, :] = t[64 * e + 24 : 64 * e + 48]
        hsend[h, :, 0:128] = hstage[0].astype(bf16)
        hsend[h, :, 128:256] = hstage[1].astype(bf16)

    def send_rows(h, dst, k):
        @pl.when(self_source)
        def _():
            local(h, dst, k).start()
            direct(h, dst, k, 0).start()
            direct(h, dst, k, 1).start()

        @pl.when(far_source)
        def _():
            first(h, dst, k).start()

        if h == 0 and isinstance(k, int):

            @pl.when(offset == 0)
            def _():
                direct(h, dst, k, 2).start()

    def pass_root(h, dst, k):
        @pl.when(offset == 0)
        def _():
            local(h, dst, k).wait()

        @pl.when(far_source)
        def _():
            onward(h, dst, k, 0).start()
            onward(h, dst, k, 1).start()

    def pass_side(h, dst, k):
        @pl.when((offset == 1) | (offset == 3))
        def _():
            local(h, dst, k).wait()

        @pl.when((offset == 1) & (lax.rem(k, 2) == 0) & ((k > 0) | (h > 0)))
        def _():
            onward(h, dst, k, 0).start()

        @pl.when((offset == 3) & (lax.rem(k, 2) == 1))
        def _():
            onward(h, dst, k, 1).start()

    def pass_far(h, dst, k):
        @pl.when(offset == 2)
        def _():
            local(h, dst, k).wait()

    low = lane < 64
    zero = jnp.zeros((128, 128), f32)

    def spread(h, dst):
        for b in range(16):
            q_ = flat[h, 32 + b].astype(f32)
            r_ = pltpu.roll(q_, 64, axis=1)
            dst[b, 0:128] = jnp.where(low, q_, zero).astype(bf16)
            dst[b, 128:256] = jnp.where(low, zero, r_).astype(bf16)
            dst[b + 16, 0:128] = jnp.where(low, r_, zero).astype(bf16)
            dst[b + 16, 128:256] = jnp.where(low, zero, q_).astype(bf16)

    def twice(ref, rows=slice(None)):
        v = ref[rows, :]
        return jnp.concatenate([v, v], axis=1)

    def outer_unit(k, d, slot_, bp):
        lref, rref, half = ((hl, r1f, 1), (hr, r1m, 0))[d]
        both = lref[pl.ds(pl.multiple_of(k * 128, 128), 128), :]
        lhs0 = jnp.concatenate([both[:, 0:128], both[:, 128:256]], axis=0)
        b0, b1 = 2 * bp, 2 * bp + 1
        rhs0 = jnp.concatenate([flat[half, b0], flat[half, b1]], axis=1)
        o0 = jnp.dot(lhs0, rhs0, preferred_element_type=f32).astype(bf16)
        rhs1 = jnp.concatenate([rref[b0], rref[b1]], axis=1)
        o1 = jnp.dot(both, rhs1, preferred_element_type=f32).astype(bf16)
        for e, b in enumerate((b0, b1)):
            rows = slice(b * 32, b * 32 + 32)
            lanes = slice(e * 128, e * 128 + 128)
            for i in range(8):
                pbuf[slot_, rows, i * 128 : i * 128 + 128] = o0[i * 32 : i * 32 + 32, lanes]
            for i in range(4):
                pbuf[slot_, rows, (8 + i) * 128 : (9 + i) * 128] = o1[i * 32 : i * 32 + 32, lanes]

    def project_chunk(k, d, slot_, n):
        cols = slice(n * 256, n * 256 + 256)
        z_ = jnp.dot((wf, wm)[d][...], pbuf[slot_, :, cols], preferred_element_type=f32)
        z_ = jnp.maximum(z_ + twice(bout_b), 0.0)
        zbuf[k, :, cols] = z_ if d == 0 else zbuf[k, :, cols] + z_

    def norm_chunk(k, n):
        pair = zbuf[k, :, n * 256 : n * 256 + 256]
        mean = jnp.mean(pair, axis=0, keepdims=True)
        cen = pair - mean
        var = jnp.mean(cen * cen, axis=0, keepdims=True)
        nbuf[n % 2] = (cen * lax.rsqrt(var + EPSILON) * twice(pg_b) + twice(pb_b)).astype(bf16)

    def up_chunk(n, part):
        rows = slice(part * 128, part * 128 + 128)
        hid = jnp.dot(wup[rows, :], nbuf[n % 2], preferred_element_type=f32)
        hbuf[n % 2, rows, :] = jnp.maximum(hid + twice(bup_b, rows), 0.0).astype(bf16)

    def down_chunk(k, n):
        upd = jnp.dot(wdn[...], hbuf[n % 2], preferred_element_type=f32)
        res = zbuf[k, :, n * 256 : n * 256 + 256] + upd + twice(bdn_b)
        for e in range(2):
            c = 2 * n + e
            t = res[:, e * 128 : e * 128 + 128].T.astype(bf16)
            for q_ in range(4):
                if c < 8:
                    out[c // 4, 4 * k + c % 4, 48 * q_ : 48 * q_ + 32, :] = t[32 * q_ : 32 * q_ + 32]
                else:
                    out[0, 4 * k + c - 8, 48 * q_ + 32 : 48 * q_ + 48, :] = t[16 * q_ : 16 * q_ + 16]
                    out[1, 4 * k + c - 8, 48 * q_ + 32 : 48 * q_ + 48, :] = t[64 + 16 * q_ : 80 + 16 * q_]

    def outer(k, d, slot_):
        return [functools.partial(outer_unit, k, d, slot_, bp) for bp in range(16)]

    def project(k, d, slot_):
        return [functools.partial(project_chunk, k, d, slot_, n) for n in range(6)]

    def transition(k):
        stages = []
        for n in range(0, 6, 2):
            both = (n, n + 1)
            stages += [functools.partial(norm_chunk, k, m) for m in both]
            for part in range(4):
                stages += [functools.partial(up_chunk, m, part) for m in both]
            stages += [functools.partial(down_chunk, k, m) for m in both]
        return stages

    def interleave(*lists):
        steps = [((i + 0.5) / len(l), j, f) for j, l in enumerate(lists) for i, f in enumerate(l)]
        for _, _, f in sorted(steps, key=lambda t: t[:2]):
            f()

    shared(0).wait_recv()

    @pl.when(offset == 0)
    def _():
        make_rows(0)
        send_rows(0, hl, 0)

    for dz in (0, -1, 1, -2, 2, -3):
        got_over(1, dz)
        share(1, 1 - ylo, dz)
    spread(0, r1m)
    for dz in (3, -4):
        got_over(1, dz)
        share(1, 1 - ylo, dz)
    pass_root(0, hl, 0)
    shared(1).wait_recv()
    spread(1, r1f)

    @pl.when(offset == 0)
    def _():
        make_rows(1)

    def send_left(k):
        @pl.when(offset == 0)
        def _():
            send_rows(0, hl, k)

    def send_right(k):
        @pl.when(offset == 0)
        def _():
            send_rows(1, hr, k)

    pass_side(0, hl, 0)
    pass_far(0, hl, 0)
    send_left(jnp.int32(1))
    interleave(outer(0, 0, 0))

    def left_step(k, parity):
        pass_root(0, hl, k)
        pass_side(0, hl, k)
        pass_far(0, hl, k)

        @pl.when(k < 5)
        def _():
            send_left(k + 1)

        if parity == 1:
            send_right((k - 1) // 2)

            @pl.when(k >= 3)
            def _():
                pass_root(1, hr, (k - 3) // 2)

            @pl.when(k >= 5)
            def _():
                pass_side(1, hr, (k - 5) // 2)

        interleave(outer(k, 0, parity), project(k - 1, 0, 1 - parity))

    def left_pair(t, carry):
        left_step(2 * t + 1, 1)
        left_step(2 * t + 2, 0)
        return carry

    lax.fori_loop(0, 2, left_pair, 0)
    left_step(jnp.int32(5), 1)

    one = jnp.int32(1)
    send_right(3 * one)
    pass_root(1, hr, 2 * one)
    pass_side(1, hr, one)
    pass_far(1, hr, 0 * one)
    interleave(outer(0, 1, 0), project(5, 0, 1))
    send_right(4 * one)
    pass_root(1, hr, 3 * one)
    pass_side(1, hr, 2 * one)
    pass_far(1, hr, one)
    interleave(outer(1, 1, 1), project(0, 1, 0))

    def right_step(k, parity):
        @pl.when(k == 1)
        def _():
            send_right(5 * one)

        @pl.when(k < 3)
        def _():
            pass_root(1, hr, k + 3)

        @pl.when(k < 4)
        def _():
            pass_side(1, hr, k + 2)

        pass_far(1, hr, k + 1)
        interleave(outer(k + 1, 1, 1 - parity), project(k, 1, parity), transition(k - 1))

    def right_pair(t, carry):
        right_step(2 * t + 1, 1)
        right_step(2 * t + 2, 0)
        return carry

    lax.fori_loop(0, 2, right_pair, 0)
    interleave(project(5, 1, 1), transition(4))
    interleave(transition(5))

    for h, dst in ((0, hl), (1, hr)):
        for k in range(6):

            @pl.when(far_source)
            def _(h=h, dst=dst, k=k):
                first(h, dst, k).wait_send()

            @pl.when(offset == 0)
            def _(h=h, dst=dst, k=k):
                for way in range(3 if k + h == 0 else 2):
                    direct(h, dst, k, way).wait_send()

            if k + h > 0:

                @pl.when(offset == (1, 3)[k % 2])
                def _(h=h, dst=dst, k=k):
                    onward(h, dst, k, k % 2).wait_send()

    for h in range(2):
        shared(h).wait_send()
    for c in sent:
        c.wait_send()


def fused(x, *params):
    rows = x.shape[0]
    bf16, f32 = jnp.bfloat16, jnp.float32
    dma = pltpu.SemaphoreType.DMA
    args = (x,) + tuple(p[None, :] if p.ndim == 1 else p for p in params)
    args = tuple(pltpu.with_memory_space_constraint(a, pltpu.HBM) for a in args)
    out_bytes = 2 * 24 * 192 * 128 * 2
    out = pl.pallas_call(
        fused_kernel,
        in_specs=[pl.BlockSpec(memory_space=pltpu.HBM)] * len(args),
        out_specs=pl.BlockSpec(memory_space=pltpu.VMEM),
        out_shape=jax.ShapeDtypeStruct((2, 24, 192, 128), bf16),
        scratch_shapes=[pltpu.VMEM(a.shape, a.dtype) for a in args] + [
            dma((len(args),)),
            pltpu.VMEM((2, 48, 32, rows, 128), bf16),
            pltpu.VMEM((768, 256), bf16),
            pltpu.VMEM((768, 256), bf16),
            pltpu.VMEM((2, 48, rows, 128), f32),
            pltpu.VMEM((2, 48, rows, 128), bf16),
            pltpu.VMEM((2, 768, 128), f32),
            pltpu.VMEM((2, 768, 256), bf16),
            pltpu.VMEM((32, 256, 128), bf16),
            pltpu.VMEM((32, 256, 128), bf16),
            pltpu.VMEM((2, 1024, 1536), bf16),
            pltpu.VMEM((6, 128, 1536), f32),
            pltpu.VMEM((2, 128, 256), bf16),
            pltpu.VMEM((2, 512, 256), bf16),
            pltpu.VMEM((1024, 128), f32),
            pltpu.VMEM((128, 1024), bf16),
            pltpu.VMEM((128, 1024), bf16),
            pltpu.VMEM((512, 128), bf16),
            pltpu.VMEM((128, 512), bf16),
            pltpu.VMEM((128, 128), f32),
            pltpu.VMEM((128, 128), f32),
            pltpu.VMEM((128, 128), f32),
            pltpu.VMEM((128, 128), f32),
            pltpu.VMEM((512, 128), f32),
            dma((2,)),
            dma((2, 8)),
            dma((2, 8)),
            dma((2, 8)),
            dma((2, 8)),
            dma((2,)),
            dma((2,)),
            dma((2, 6)),
            dma((2, 3, 6)),
            dma((2, 6)),
        ],
        compiler_params=pltpu.CompilerParams(
            collective_id=0, has_side_effects=True, vmem_limit_bytes=48 * 1024 * 1024
        ),
        name="fused",
    )(*args)
    return out.reshape(48, 192, 128)


def shards(
    alignment,
    alignment_norm_gain,
    alignment_norm_bias,
    projection_weight,
    projection_bias_pair,
    *rest,
):
    return fused(
        alignment,
        alignment_norm_gain,
        alignment_norm_bias,
        projection_weight.T,
        projection_bias_pair,
        *rest,
    )


def solution(mesh):
    return jax.shard_map(
        shards,
        mesh=mesh,
        in_specs=(P("row", "col", None),) + (P(),) * 12,
        out_specs=P("row", "col", None),
        check_vma=False,
    )
```

```python
import functools

import jax
import jax.numpy as jnp
from jax import lax
from jax.experimental import pallas as pl
from jax.experimental.pallas import tpu as pltpu
from jax.sharding import PartitionSpec as P

EPSILON = 1e-05
VMEM_LIMIT = 60 * 1024 * 1024


MESH = pl.DeviceIdType.MESH
ZN, XN = 8, 4


def project_block(x_ref, gain_ref, bias_ref, w_ref, pbias_ref, stage):
    rows = x_ref.shape[0]
    low = lax.broadcasted_iota(jnp.int32, (1, 128), 1) < 64
    w2 = jnp.concatenate([w_ref[...], w_ref[...]], axis=0)
    pbias = jnp.concatenate([pbias_ref[...], pbias_ref[...]], axis=1)
    for s in range(rows):
        x = x_ref[s].astype(jnp.float32)
        mean = jnp.mean(x, axis=-1, keepdims=True)
        cen = x - mean
        var = jnp.mean(cen * cen, axis=-1, keepdims=True)
        normed = (cen * lax.rsqrt(var + EPSILON) * gain_ref[...] + bias_ref[...]).astype(jnp.bfloat16)
        d = lax.dot_general(normed, w2, (((1,), (1,)), ((), ())), preferred_element_type=jnp.float32)
        d = d + pbias
        t0 = jnp.concatenate([d[48 * q : 48 * q + 32] for q in range(4)], axis=0).T
        t1 = jnp.concatenate([d[48 * q + 32 : 48 * q + 48] for q in range(4)] * 2, axis=0).T
        for h in range(2):
            stage[h, 0:32, s, :] = t0[32 * h : 32 * h + 32]
            stage[h, 32:48, s, :] = jnp.where(low, t1[32 * h : 32 * h + 16], t1[32 * h + 16 : 32 * h + 32])


def fused_kernel(
    *refs,
):
    ins, vins = refs[:13], refs[14:27]
    out = refs[13]
    in_sem = refs[27]
    fetch = [pltpu.make_async_copy(a, v, in_sem.at[i]) for i, (a, v) in enumerate(zip(ins, vins))]
    for c in fetch:
        c.start()
    fused_body(fetch, *vins, out, *refs[28:])


def fused_body(
    fetch, x_ref, gain_ref, bias_ref, w_ref, pbias_ref, w_out, bout, pg, pb, w_up, bup, w_down, bdn, out,
    g, hl, hr, stage, block, hstage, hsend, r1f, r1m, pbuf, zbuf, nbuf, hbuf, wtmp,
    wf, wm, wup, wdn, bout_b, pg_b, pb_b, bdn_b, bup_b,
    own_sem, f_send, f_recv, z_send, z_recv, y_send, y_recv, p_send, p_recv, hs_sem, hf_sem, h_recv,
):
    bf16, f32 = jnp.bfloat16, jnp.float32

    def prepare_weights():
        total = 4 * 32
        wtmp[...] = w_out[...].astype(f32) * (1.0 / total)
        for m in range(8):
            rows = slice(m * 128, m * 128 + 128)
            wm[:, rows] = wtmp[rows, :].T.astype(bf16)
            picked = [wtmp[pl.ds(4 * m + e, 32, stride=32), :] for e in range(4)]
            wf[:, rows] = jnp.concatenate(picked, axis=0).T.astype(bf16)
        for m in range(4):
            rows = slice(m * 128, m * 128 + 128)
            wup[rows, :] = w_up[:, rows].astype(f32).T.astype(bf16)
            wdn[:, rows] = w_down[rows, :].astype(f32).T.astype(bf16)
            bup_b[rows, :] = jnp.broadcast_to(bup[:, rows], (128, 128)).T
        for wide, narrow in ((bout_b, bout), (pg_b, pg), (pb_b, pb), (bdn_b, bdn)):
            wide[...] = jnp.broadcast_to(narrow[...], (128, 128)).T

    row, col = lax.axis_index("row"), lax.axis_index("col")
    core = lax.rem(row, 2)
    z = lax.rem(row // 2, ZN)
    ylo = row // (2 * ZN)
    x = lax.rem(col, XN)
    yhi = col // XN

    def row_of(ylo_, z_, core_):
        return (ylo_ * ZN + z_) * 2 + core_

    zup, zdn = lax.rem(z + 1, ZN), lax.rem(z + ZN - 1, ZN)
    up = (row_of(ylo, zup, core), col)
    down = (row_of(ylo, zdn, core), col)
    across = (row_of(1 - ylo, z, core), col)
    partner = (row_of(ylo, z, 1 - core), col)
    xup = (row, yhi * XN + lax.rem(x + 1, XN))
    xdn = (row, yhi * XN + lax.rem(x + XN - 1, XN))
    facing = (row_of(1 - ylo, z, core), (1 - yhi) * XN + x)

    barrier = pltpu.get_barrier_semaphore()
    far = (row, yhi * XN + lax.rem(x + 2, XN))
    diagonal = [(facing[0], (1 - yhi) * XN + lax.rem(x + d, XN)) for d in range(1, XN)]
    near2 = [(row_of(ylo, lax.rem(z + d, ZN), core), col) for d in (2, ZN - 2)]
    others = (up, down, *near2, across, partner, xup, xdn, far, facing, *diagonal)
    for dev in others:
        pl.semaphore_signal(barrier, inc=1, device_id=dev, device_id_type=MESH)

    for c in fetch[:5]:
        c.wait()
    project_block(x_ref, gain_ref, bias_ref, w_ref, pbias_ref, stage)
    block[...] = stage[...].astype(bf16)
    own = [pltpu.make_async_copy(block.at[h], g.at[h, :, row], own_sem.at[h]) for h in range(2)]
    for c in own:
        c.start()
    pl.semaphore_wait(barrier, len(others))

    sent = []

    def slot(h, ylo_, dz, core_):
        return g.at[h, :, row_of(ylo_, lax.rem(z + dz + ZN, ZN), core_)]

    def copy(ref, send, recv, dev):
        c = pltpu.make_async_remote_copy(ref, ref, send, recv, device_id=dev, device_id_type=MESH)
        return c

    def send(ref, s, r, dev):
        c = copy(ref, s, r, dev)
        c.start()
        sent.append(c)

    def arrived(ref, r):
        copy(ref, own_sem.at[0], r, partner).wait_recv()

    up2 = (row_of(ylo, lax.rem(z + 2, ZN), core), col)
    down2 = (row_of(ylo, lax.rem(z + ZN - 2, ZN), core), col)

    def along(h, dz, there, dev):
        send(slot(h, ylo, dz, core), z_send.at[h, there + 4], z_recv.at[h, there + 4], dev)

    def got(h, dz):
        arrived(slot(h, ylo, dz, core), z_recv.at[h, dz + 4])

    def over(h, dz):
        send(slot(h, ylo, dz, core), y_send.at[h, dz + 4], y_recv.at[h, dz + 4], across)

    def got_over(h, dz):
        arrived(slot(h, 1 - ylo, dz, core), y_recv.at[h, dz + 4])

    def share(h, ylo_, dz):
        copy(slot(h, ylo_, dz, core), p_send.at[h], p_recv.at[h], partner).start()

    def shared(h):
        whole = g.at[h, 0:24]
        return copy(whole, p_send.at[h], p_recv.at[h], partner)

    def along_facing(there, dev):
        send(slot(0, 1 - ylo, 0, core), f_send.at[there + 4], f_recv.at[there + 4], dev)

    def got_facing(dz):
        arrived(slot(0, 1 - ylo, dz, core), f_recv.at[dz + 4])

    own[0].wait()
    over(0, 0)
    along(0, 0, -1, up)
    along(0, 0, 1, down)
    along(0, 0, -2, up2)
    along(0, 0, 2, down2)
    share(0, ylo, 0)
    own[1].wait()
    along(1, 0, -1, up)
    along(1, 0, 1, down)
    over(1, 0)
    share(1, ylo, 0)
    for c in fetch[5:]:
        c.wait()
    prepare_weights()
    got_over(0, 0)
    along_facing(-1, up)
    along_facing(1, down)
    along_facing(-2, up2)
    along_facing(2, down2)
    share(0, 1 - ylo, 0)
    for dz in (-1, 1):
        got(0, dz)
        share(0, ylo, dz)
    got(0, -2)
    along(0, -2, -3, up)
    along(0, -2, -4, up2)
    share(0, ylo, -2)
    got(0, 2)
    along(0, 2, 3, down)
    share(0, ylo, 2)
    for dz in (-1, 1):
        got(1, dz)
        along(1, dz, dz * 2, up if dz < 0 else down)
        over(1, dz)
        share(1, ylo, dz)
    for dz in (-3, 3, -4):
        got(0, dz)
        over(0, dz)
        share(0, ylo, dz)
    for dz in (-2, 2):
        got(1, dz)
        along(1, dz, dz * 3 // 2, up if dz < 0 else down)
        over(1, dz)
        share(1, ylo, dz)
    for dz in (-1, 1, -2, 2):
        got_facing(dz)
        share(0, 1 - ylo, dz)
    got(1, -3)
    along(1, -3, -4, up)
    over(1, -3)
    share(1, ylo, -3)
    got(1, 3)
    over(1, 3)
    share(1, ylo, 3)
    for dz in (-3, 3, -4):
        got_over(0, dz)
        share(0, 1 - ylo, dz)
    got(1, -4)
    over(1, -4)
    share(1, ylo, -4)
    for dz in (0, -1, 1):
        got_over(1, dz)
        share(1, 1 - ylo, dz)

    offset = lax.rem(x - z // 2 + XN, XN)
    q = lax.rem(row, 4)
    shift0 = lax.rem(128 - 32 * q, 128)
    shift1 = lax.rem(128 - 32 * q + 64, 128)
    shift2 = lax.rem(128 - 16 * q + 32, 128)
    lane = lax.broadcasted_iota(jnp.int32, (1, 128), 1)
    flat = g.reshape(2, 48, 128, 128)
    self_source = (offset == 0) & (ylo == yhi)
    far_source = (offset == 0) & (ylo != yhi)

    def chunk(ref, k):
        return ref.at[pl.ds(pl.multiple_of(k * 128, 128), 128)]

    def local(h, dst, k):
        return pltpu.make_async_copy(chunk(hsend.at[h], k), chunk(dst, k), h_recv.at[h, k])

    def first(h, dst, k):
        return pltpu.make_async_remote_copy(
            chunk(hsend.at[h], k), chunk(dst, k), hs_sem.at[h, k], h_recv.at[h, k], device_id=facing, device_id_type=MESH
        )

    def direct(h, dst, k, way):
        step_ = (1, XN - 1, 2)[way]
        dev = (jnp.where(ylo == yhi, row, facing[0]), jnp.where(ylo == yhi, yhi, 1 - yhi) * XN + lax.rem(x + step_, XN))
        return pltpu.make_async_remote_copy(
            chunk(hsend.at[h], k), chunk(dst, k), hf_sem.at[h, way, k], h_recv.at[h, k], device_id=dev, device_id_type=MESH
        )

    def onward(h, dst, k, way):
        return copy(chunk(dst, k), hf_sem.at[h, way, k], h_recv.at[h, k], (xup, xdn)[way])

    def make_rows(h):
        for p in range(16):
            a0 = pltpu.roll(flat[h, p].astype(f32), shift0, axis=1)
            a1 = pltpu.roll(flat[h, p + 16].astype(f32), shift1, axis=1)
            b = pltpu.roll(flat[h, 32 + p].astype(f32), shift2, axis=1)
            t = jnp.where(lane < 32, a0, jnp.where((lane >= 64) & (lane < 96), a1, b)).T
            for e in range(2):
                at = pl.ds(p + 16 * e, 24, stride=32)
                hstage[0, at, :] = t[64 * e : 64 * e + 24]
                hstage[1, at, :] = t[64 * e + 24 : 64 * e + 48]
        hsend[h, :, 0:128] = hstage[0].astype(bf16)
        hsend[h, :, 128:256] = hstage[1].astype(bf16)

    def send_rows(h, dst, k):
        @pl.when(self_source)
        def _():
            local(h, dst, k).start()
            direct(h, dst, k, 0).start()
            direct(h, dst, k, 1).start()

        @pl.when(far_source)
        def _():
            first(h, dst, k).start()

        if h == 0 and isinstance(k, int):

            @pl.when(offset == 0)
            def _():
                direct(h, dst, k, 2).start()

    def pass_root(h, dst, k):
        @pl.when(offset == 0)
        def _():
            local(h, dst, k).wait()

        @pl.when(far_source)
        def _():
            onward(h, dst, k, 0).start()
            onward(h, dst, k, 1).start()

    def pass_side(h, dst, k):
        @pl.when((offset == 1) | (offset == 3))
        def _():
            local(h, dst, k).wait()

        @pl.when((offset == 1) & (lax.rem(k, 2) == 0) & ((k > 0) | (h > 0)))
        def _():
            onward(h, dst, k, 0).start()

        @pl.when((offset == 3) & (lax.rem(k, 2) == 1))
        def _():
            onward(h, dst, k, 1).start()

    def pass_far(h, dst, k):
        @pl.when(offset == 2)
        def _():
            local(h, dst, k).wait()

    low = lane < 64
    zero = jnp.zeros((128, 128), f32)

    def spread(h, dst):
        for b in range(16):
            q_ = flat[h, 32 + b].astype(f32)
            r_ = pltpu.roll(q_, 64, axis=1)
            dst[b, 0:128] = jnp.where(low, q_, zero).astype(bf16)
            dst[b, 128:256] = jnp.where(low, zero, r_).astype(bf16)
            dst[b + 16, 0:128] = jnp.where(low, r_, zero).astype(bf16)
            dst[b + 16, 128:256] = jnp.where(low, zero, q_).astype(bf16)

    def twice(ref, rows=slice(None)):
        v = ref[rows, :]
        return jnp.concatenate([v, v], axis=1)

    def outer_unit(k, d, slot_, bp):
        lref, rref, half = ((hl, r1f, 1), (hr, r1m, 0))[d]
        both = lref[pl.ds(pl.multiple_of(k * 128, 128), 128), :]
        lhs0 = jnp.concatenate([both[:, 0:128], both[:, 128:256]], axis=0)
        b0, b1 = 2 * bp, 2 * bp + 1
        rhs0 = jnp.concatenate([flat[half, b0], flat[half, b1]], axis=1)
        o0 = jnp.dot(lhs0, rhs0, preferred_element_type=f32).astype(bf16)
        rhs1 = jnp.concatenate([rref[b0], rref[b1]], axis=1)
        o1 = jnp.dot(both, rhs1, preferred_element_type=f32).astype(bf16)
        for e, b in enumerate((b0, b1)):
            rows = slice(b * 32, b * 32 + 32)
            lanes = slice(e * 128, e * 128 + 128)
            for i in range(8):
                pbuf[slot_, rows, i * 128 : i * 128 + 128] = o0[i * 32 : i * 32 + 32, lanes]
            for i in range(4):
                pbuf[slot_, rows, (8 + i) * 128 : (9 + i) * 128] = o1[i * 32 : i * 32 + 32, lanes]

    def project_chunk(k, d, slot_, n):
        cols = slice(n * 256, n * 256 + 256)
        z_ = jnp.dot((wf, wm)[d][...], pbuf[slot_, :, cols], preferred_element_type=f32)
        z_ = jnp.maximum(z_ + twice(bout_b), 0.0)
        zbuf[k, :, cols] = z_ if d == 0 else zbuf[k, :, cols] + z_

    def norm_chunk(k, n):
        pair = zbuf[k, :, n * 256 : n * 256 + 256]
        mean = jnp.mean(pair, axis=0, keepdims=True)
        cen = pair - mean
        var = jnp.mean(cen * cen, axis=0, keepdims=True)
        nbuf[n % 2] = (cen * lax.rsqrt(var + EPSILON) * twice(pg_b) + twice(pb_b)).astype(bf16)

    def up_chunk(n, part):
        rows = slice(part * 128, part * 128 + 128)
        hid = jnp.dot(wup[rows, :], nbuf[n % 2], preferred_element_type=f32)
        hbuf[n % 2, rows, :] = jnp.maximum(hid + twice(bup_b, rows), 0.0).astype(bf16)

    def down_chunk(k, n):
        upd = jnp.dot(wdn[...], hbuf[n % 2], preferred_element_type=f32)
        res = zbuf[k, :, n * 256 : n * 256 + 256] + upd + twice(bdn_b)
        for e in range(2):
            c = 2 * n + e
            t = res[:, e * 128 : e * 128 + 128].T.astype(bf16)
            for q_ in range(4):
                if c < 8:
                    out[c // 4, 4 * k + c % 4, 48 * q_ : 48 * q_ + 32, :] = t[32 * q_ : 32 * q_ + 32]
                else:
                    out[0, 4 * k + c - 8, 48 * q_ + 32 : 48 * q_ + 48, :] = t[16 * q_ : 16 * q_ + 16]
                    out[1, 4 * k + c - 8, 48 * q_ + 32 : 48 * q_ + 48, :] = t[64 + 16 * q_ : 80 + 16 * q_]

    def outer(k, d, slot_):
        return [functools.partial(outer_unit, k, d, slot_, bp) for bp in range(16)]

    def project(k, d, slot_):
        return [functools.partial(project_chunk, k, d, slot_, n) for n in range(6)]

    def transition(k):
        stages = []
        for n in range(0, 6, 2):
            both = (n, n + 1)
            stages += [functools.partial(norm_chunk, k, m) for m in both]
            for part in range(4):
                stages += [functools.partial(up_chunk, m, part) for m in both]
            stages += [functools.partial(down_chunk, k, m) for m in both]
        return stages

    def interleave(*lists):
        steps = [((i + 0.5) / len(l), j, f) for j, l in enumerate(lists) for i, f in enumerate(l)]
        for _, _, f in sorted(steps, key=lambda t: t[:2]):
            f()

    one = jnp.int32(1)
    shared(0).wait_recv()

    @pl.when(offset == 0)
    def _():
        make_rows(0)
        send_rows(0, hl, 0)

    for dz in (-2, 2):
        got_over(1, dz)
        share(1, 1 - ylo, dz)
    spread(0, r1m)

    @pl.when(offset == 0)
    def _():
        send_rows(0, hl, one)

    for dz in (-3, 3, -4):
        got_over(1, dz)
        share(1, 1 - ylo, dz)
    pass_root(0, hl, 0)
    shared(1).wait_recv()
    spread(1, r1f)

    @pl.when(offset == 0)
    def _():
        send_rows(0, hl, 2 * one)
        make_rows(1)

    def send_left(k):
        @pl.when(offset == 0)
        def _():
            send_rows(0, hl, k)

    def send_right(k):
        @pl.when(offset == 0)
        def _():
            send_rows(1, hr, k)

    pass_side(0, hl, 0)
    pass_far(0, hl, 0)
    send_left(3 * one)
    interleave(outer(0, 0, 0))

    def left_step(k, parity):
        pass_root(0, hl, k)
        pass_side(0, hl, k)
        pass_far(0, hl, k)

        @pl.when(k < 3)
        def _():
            send_left(k + 3)

        send_right(k - 1)

        @pl.when(k >= 3)
        def _():
            pass_root(1, hr, k - 3)

        @pl.when(k >= 5)
        def _():
            pass_side(1, hr, k - 5)

        interleave(outer(k, 0, parity), project(k - 1, 0, 1 - parity))

    def left_pair(t, carry):
        left_step(2 * t + 1, 1)
        left_step(2 * t + 2, 0)
        return carry

    lax.fori_loop(0, 2, left_pair, 0)
    left_step(jnp.int32(5), 1)

    send_right(5 * one)
    pass_root(1, hr, 3 * one)
    pass_side(1, hr, one)
    pass_far(1, hr, 0 * one)
    interleave(outer(0, 1, 0), project(5, 0, 1))
    pass_root(1, hr, 4 * one)
    pass_side(1, hr, 2 * one)
    pass_far(1, hr, one)
    interleave(outer(1, 1, 1), project(0, 1, 0))

    def right_step(k, parity):
        @pl.when(k == 1)
        def _():
            pass_root(1, hr, k + 4)

        @pl.when(k < 4)
        def _():
            pass_side(1, hr, k + 2)

        pass_far(1, hr, k + 1)
        interleave(outer(k + 1, 1, 1 - parity), project(k, 1, parity), transition(k - 1))

    def right_pair(t, carry):
        right_step(2 * t + 1, 1)
        right_step(2 * t + 2, 0)
        return carry

    lax.fori_loop(0, 2, right_pair, 0)
    interleave(project(5, 1, 1), transition(4))
    interleave(transition(5))

    for h, dst in ((0, hl), (1, hr)):
        for k in range(6):

            @pl.when(far_source)
            def _(h=h, dst=dst, k=k):
                first(h, dst, k).wait_send()

            @pl.when(offset == 0)
            def _(h=h, dst=dst, k=k):
                for way in range(3 if k + h == 0 else 2):
                    direct(h, dst, k, way).wait_send()

            if k + h > 0:

                @pl.when(offset == (1, 3)[k % 2])
                def _(h=h, dst=dst, k=k):
                    onward(h, dst, k, k % 2).wait_send()

    for h in range(2):
        shared(h).wait_send()
    for c in sent:
        c.wait_send()


def fused(x, *params):
    rows = x.shape[0]
    bf16, f32 = jnp.bfloat16, jnp.float32
    dma = pltpu.SemaphoreType.DMA
    args = (x,) + tuple(p[None, :] if p.ndim == 1 else p for p in params)
    args = tuple(pltpu.with_memory_space_constraint(a, pltpu.HBM) for a in args)
    out_bytes = 2 * 24 * 192 * 128 * 2
    out = pl.pallas_call(
        fused_kernel,
        in_specs=[pl.BlockSpec(memory_space=pltpu.HBM)] * len(args),
        out_specs=pl.BlockSpec(memory_space=pltpu.VMEM),
        out_shape=jax.ShapeDtypeStruct((2, 24, 192, 128), bf16),
        scratch_shapes=[pltpu.VMEM(a.shape, a.dtype) for a in args] + [
            dma((len(args),)),
            pltpu.VMEM((2, 48, 32, rows, 128), bf16),
            pltpu.VMEM((768, 256), bf16),
            pltpu.VMEM((768, 256), bf16),
            pltpu.VMEM((2, 48, rows, 128), f32),
            pltpu.VMEM((2, 48, rows, 128), bf16),
            pltpu.VMEM((2, 768, 128), f32),
            pltpu.VMEM((2, 768, 256), bf16),
            pltpu.VMEM((32, 256, 128), bf16),
            pltpu.VMEM((32, 256, 128), bf16),
            pltpu.VMEM((2, 1024, 1536), bf16),
            pltpu.VMEM((6, 128, 1536), f32),
            pltpu.VMEM((2, 128, 256), bf16),
            pltpu.VMEM((2, 512, 256), bf16),
            pltpu.VMEM((1024, 128), f32),
            pltpu.VMEM((128, 1024), bf16),
            pltpu.VMEM((128, 1024), bf16),
            pltpu.VMEM((512, 128), bf16),
            pltpu.VMEM((128, 512), bf16),
            pltpu.VMEM((128, 128), f32),
            pltpu.VMEM((128, 128), f32),
            pltpu.VMEM((128, 128), f32),
            pltpu.VMEM((128, 128), f32),
            pltpu.VMEM((512, 128), f32),
            dma((2,)),
            dma((8,)),
            dma((8,)),
            dma((2, 8)),
            dma((2, 8)),
            dma((2, 8)),
            dma((2, 8)),
            dma((2,)),
            dma((2,)),
            dma((2, 6)),
            dma((2, 3, 6)),
            dma((2, 6)),
        ],
        compiler_params=pltpu.CompilerParams(
            collective_id=0, has_side_effects=True, vmem_limit_bytes=48 * 1024 * 1024
        ),
        name="fused",
    )(*args)
    return out.reshape(48, 192, 128)


def shards(
    alignment,
    alignment_norm_gain,
    alignment_norm_bias,
    projection_weight,
    projection_bias_pair,
    *rest,
):
    return fused(
        alignment,
        alignment_norm_gain,
        alignment_norm_bias,
        projection_weight.T,
        projection_bias_pair,
        *rest,
    )


def solution(mesh):
    return jax.shard_map(
        shards,
        mesh=mesh,
        in_specs=(P("row", "col", None),) + (P(),) * 12,
        out_specs=P("row", "col", None),
        check_vma=False,
    )
```

```python
import functools

import jax
import jax.numpy as jnp
from jax import lax
from jax.experimental import pallas as pl
from jax.experimental.pallas import tpu as pltpu
from jax.sharding import PartitionSpec as P

EPSILON = 1e-05
VMEM_LIMIT = 60 * 1024 * 1024


MESH = pl.DeviceIdType.MESH
ZN, XN = 8, 4


def project_block(x_ref, gain_ref, bias_ref, w_ref, pbias_ref, stage):
    rows = x_ref.shape[0]
    low = lax.broadcasted_iota(jnp.int32, (1, 128), 1) < 64
    w2 = jnp.concatenate([w_ref[...], w_ref[...]], axis=0)
    pbias = jnp.concatenate([pbias_ref[...], pbias_ref[...]], axis=1)
    for s in range(rows):
        x = x_ref[s].astype(jnp.float32)
        mean = jnp.mean(x, axis=-1, keepdims=True)
        cen = x - mean
        var = jnp.mean(cen * cen, axis=-1, keepdims=True)
        normed = (cen * lax.rsqrt(var + EPSILON) * gain_ref[...] + bias_ref[...]).astype(jnp.bfloat16)
        d = lax.dot_general(normed, w2, (((1,), (1,)), ((), ())), preferred_element_type=jnp.float32)
        d = d + pbias
        t0 = jnp.concatenate([d[48 * q : 48 * q + 32] for q in range(4)], axis=0).T
        t1 = jnp.concatenate([d[48 * q + 32 : 48 * q + 48] for q in range(4)] * 2, axis=0).T
        for h in range(2):
            stage[h, 0:32, s, :] = t0[32 * h : 32 * h + 32]
            stage[h, 32:48, s, :] = jnp.where(low, t1[32 * h : 32 * h + 16], t1[32 * h + 16 : 32 * h + 32])


def fused_kernel(
    *refs,
):
    ins, vins = refs[:13], refs[14:27]
    out = refs[13]
    in_sem = refs[27]
    fetch = [pltpu.make_async_copy(a, v, in_sem.at[i]) for i, (a, v) in enumerate(zip(ins, vins))]
    for c in fetch:
        c.start()
    fused_body(fetch, *vins, out, *refs[28:])


def fused_body(
    fetch, x_ref, gain_ref, bias_ref, w_ref, pbias_ref, w_out, bout, pg, pb, w_up, bup, w_down, bdn, out,
    g, hl, hr, stage, block, hstage, hsend, r1f, r1m, pbuf, zbuf, nbuf, hbuf, wtmp,
    wf, wm, wup, wdn, bout_b, pg_b, pb_b, bdn_b, bup_b,
    own_sem, f_send, f_recv, z_send, z_recv, y_send, y_recv, p_send, p_recv, hs_sem, hf_sem, h_recv,
):
    bf16, f32 = jnp.bfloat16, jnp.float32

    def prepare_weights():
        total = 4 * 32
        wtmp[...] = w_out[...].astype(f32) * (1.0 / total)
        for m in range(8):
            rows = slice(m * 128, m * 128 + 128)
            wm[:, rows] = wtmp[rows, :].T.astype(bf16)
            picked = [wtmp[pl.ds(4 * m + e, 32, stride=32), :] for e in range(4)]
            wf[:, rows] = jnp.concatenate(picked, axis=0).T.astype(bf16)
        for m in range(4):
            rows = slice(m * 128, m * 128 + 128)
            wup[rows, :] = w_up[:, rows].astype(f32).T.astype(bf16)
            wdn[:, rows] = w_down[rows, :].astype(f32).T.astype(bf16)
            bup_b[rows, :] = jnp.broadcast_to(bup[:, rows], (128, 128)).T
        for wide, narrow in ((bout_b, bout), (pg_b, pg), (pb_b, pb), (bdn_b, bdn)):
            wide[...] = jnp.broadcast_to(narrow[...], (128, 128)).T

    row, col = lax.axis_index("row"), lax.axis_index("col")
    core = lax.rem(row, 2)
    z = lax.rem(row // 2, ZN)
    ylo = row // (2 * ZN)
    x = lax.rem(col, XN)
    yhi = col // XN

    def row_of(ylo_, z_, core_):
        return (ylo_ * ZN + z_) * 2 + core_

    zup, zdn = lax.rem(z + 1, ZN), lax.rem(z + ZN - 1, ZN)
    up = (row_of(ylo, zup, core), col)
    down = (row_of(ylo, zdn, core), col)
    across = (row_of(1 - ylo, z, core), col)
    partner = (row_of(ylo, z, 1 - core), col)
    xup = (row, yhi * XN + lax.rem(x + 1, XN))
    xdn = (row, yhi * XN + lax.rem(x + XN - 1, XN))
    facing = (row_of(1 - ylo, z, core), (1 - yhi) * XN + x)

    barrier = pltpu.get_barrier_semaphore()
    far = (row, yhi * XN + lax.rem(x + 2, XN))
    diagonal = [(facing[0], (1 - yhi) * XN + lax.rem(x + d, XN)) for d in range(1, XN)]
    near2 = [(row_of(ylo, lax.rem(z + d, ZN), core), col) for d in (2, ZN - 2)]
    others = (up, down, *near2, across, partner, xup, xdn, far, facing, *diagonal)
    for dev in others:
        pl.semaphore_signal(barrier, inc=1, device_id=dev, device_id_type=MESH)

    for c in fetch[:5]:
        c.wait()
    project_block(x_ref, gain_ref, bias_ref, w_ref, pbias_ref, stage)
    block[...] = stage[...].astype(bf16)
    own = [pltpu.make_async_copy(block.at[h], g.at[h, :, row], own_sem.at[h]) for h in range(2)]
    for c in own:
        c.start()
    pl.semaphore_wait(barrier, len(others))

    sent = []

    def slot(h, ylo_, dz, core_):
        return g.at[h, :, row_of(ylo_, lax.rem(z + dz + ZN, ZN), core_)]

    def copy(ref, send, recv, dev):
        c = pltpu.make_async_remote_copy(ref, ref, send, recv, device_id=dev, device_id_type=MESH)
        return c

    def send(ref, s, r, dev):
        c = copy(ref, s, r, dev)
        c.start()
        sent.append(c)

    def arrived(ref, r):
        copy(ref, own_sem.at[0], r, partner).wait_recv()

    up2 = (row_of(ylo, lax.rem(z + 2, ZN), core), col)
    down2 = (row_of(ylo, lax.rem(z + ZN - 2, ZN), core), col)

    def along(h, dz, there, dev):
        send(slot(h, ylo, dz, core), z_send.at[h, there + 4], z_recv.at[h, there + 4], dev)

    def got(h, dz):
        arrived(slot(h, ylo, dz, core), z_recv.at[h, dz + 4])

    def over(h, dz):
        send(slot(h, ylo, dz, core), y_send.at[h, dz + 4], y_recv.at[h, dz + 4], across)

    def got_over(h, dz):
        arrived(slot(h, 1 - ylo, dz, core), y_recv.at[h, dz + 4])

    def share(h, ylo_, dz):
        copy(slot(h, ylo_, dz, core), p_send.at[h], p_recv.at[h], partner).start()

    def shared(h):
        whole = g.at[h, 0:24]
        return copy(whole, p_send.at[h], p_recv.at[h], partner)

    own[0].wait()
    along(0, 0, -1, up)
    along(0, 0, 1, down)
    along(0, 0, -2, up2)
    along(0, 0, 2, down2)
    over(0, 0)
    share(0, ylo, 0)
    own[1].wait()
    along(1, 0, -1, up)
    along(1, 0, 1, down)
    share(1, ylo, 0)
    for c in fetch[5:]:
        c.wait()
    prepare_weights()
    for dz in (-1, 1):
        got(0, dz)
        over(0, dz)
        share(0, ylo, dz)
    got(0, -2)
    along(0, -2, -3, up)
    along(0, -2, -4, up2)
    over(0, -2)
    share(0, ylo, -2)
    got(0, 2)
    along(0, 2, 3, down)
    over(0, 2)
    share(0, ylo, 2)
    for dz in (-1, 1):
        got(1, dz)
        along(1, dz, dz * 2, up if dz < 0 else down)
        share(1, ylo, dz)
    for dz in (-3, 3, -4):
        got(0, dz)
        over(0, dz)
        share(0, ylo, dz)
    for dz in (-2, 2):
        got(1, dz)
        along(1, dz, dz * 3 // 2, up if dz < 0 else down)
        share(1, ylo, dz)
    for dz in (0, -1, 1, -2, 2):
        got_over(0, dz)
        share(0, 1 - ylo, dz)
    got(1, -3)
    along(1, -3, -4, up)
    share(1, ylo, -3)
    for dz in (-3, 3, -4):
        got_over(0, dz)
        share(0, 1 - ylo, dz)
    for dz in (0, -1, 1, -2, 2, -3):
        over(1, dz)
    got(1, 3)
    over(1, 3)
    share(1, ylo, 3)
    got(1, -4)
    over(1, -4)
    share(1, ylo, -4)

    offset = lax.rem(x - z // 2 + XN, XN)
    q = lax.rem(row, 4)
    shift0 = lax.rem(128 - 32 * q, 128)
    shift1 = lax.rem(128 - 32 * q + 64, 128)
    shift2 = lax.rem(128 - 16 * q + 32, 128)
    lane = lax.broadcasted_iota(jnp.int32, (1, 128), 1)
    flat = g.reshape(2, 48, 128, 128)
    self_source = (offset == 0) & (ylo == yhi)
    far_source = (offset == 0) & (ylo != yhi)

    def chunk(ref, k):
        return ref.at[pl.ds(pl.multiple_of(k * 128, 128), 128)]

    def local(h, dst, k):
        return pltpu.make_async_copy(chunk(hsend.at[h], k), chunk(dst, k), h_recv.at[h, k])

    def first(h, dst, k):
        return pltpu.make_async_remote_copy(
            chunk(hsend.at[h], k), chunk(dst, k), hs_sem.at[h, k], h_recv.at[h, k], device_id=facing, device_id_type=MESH
        )

    def direct(h, dst, k, way):
        step_ = (1, XN - 1, 2)[way]
        dev = (jnp.where(ylo == yhi, row, facing[0]), jnp.where(ylo == yhi, yhi, 1 - yhi) * XN + lax.rem(x + step_, XN))
        return pltpu.make_async_remote_copy(
            chunk(hsend.at[h], k), chunk(dst, k), hf_sem.at[h, way, k], h_recv.at[h, k], device_id=dev, device_id_type=MESH
        )

    def onward(h, dst, k, way):
        return copy(chunk(dst, k), hf_sem.at[h, way, k], h_recv.at[h, k], (xup, xdn)[way])

    def make_rows(h):
        for p in range(16):
            a0 = pltpu.roll(flat[h, p].astype(f32), shift0, axis=1)
            a1 = pltpu.roll(flat[h, p + 16].astype(f32), shift1, axis=1)
            b = pltpu.roll(flat[h, 32 + p].astype(f32), shift2, axis=1)
            t = jnp.where(lane < 32, a0, jnp.where((lane >= 64) & (lane < 96), a1, b)).T
            for e in range(2):
                at = pl.ds(p + 16 * e, 24, stride=32)
                hstage[0, at, :] = t[64 * e : 64 * e + 24]
                hstage[1, at, :] = t[64 * e + 24 : 64 * e + 48]
        hsend[h, :, 0:128] = hstage[0].astype(bf16)
        hsend[h, :, 128:256] = hstage[1].astype(bf16)

    def send_rows(h, dst, k):
        @pl.when(self_source)
        def _():
            local(h, dst, k).start()
            direct(h, dst, k, 0).start()
            direct(h, dst, k, 1).start()

        @pl.when(far_source)
        def _():
            first(h, dst, k).start()

        if h == 0 and isinstance(k, int):

            @pl.when(offset == 0)
            def _():
                direct(h, dst, k, 2).start()

    def pass_root(h, dst, k):
        @pl.when(offset == 0)
        def _():
            local(h, dst, k).wait()

        @pl.when(far_source)
        def _():
            onward(h, dst, k, 0).start()
            onward(h, dst, k, 1).start()

    def pass_side(h, dst, k):
        @pl.when((offset == 1) | (offset == 3))
        def _():
            local(h, dst, k).wait()

        @pl.when((offset == 1) & (lax.rem(k, 2) == 0) & ((k > 0) | (h > 0)))
        def _():
            onward(h, dst, k, 0).start()

        @pl.when((offset == 3) & (lax.rem(k, 2) == 1))
        def _():
            onward(h, dst, k, 1).start()

    def pass_far(h, dst, k):
        @pl.when(offset == 2)
        def _():
            local(h, dst, k).wait()

    low = lane < 64
    zero = jnp.zeros((128, 128), f32)

    def spread(h, dst):
        for b in range(16):
            q_ = flat[h, 32 + b].astype(f32)
            r_ = pltpu.roll(q_, 64, axis=1)
            dst[b, 0:128] = jnp.where(low, q_, zero).astype(bf16)
            dst[b, 128:256] = jnp.where(low, zero, r_).astype(bf16)
            dst[b + 16, 0:128] = jnp.where(low, r_, zero).astype(bf16)
            dst[b + 16, 128:256] = jnp.where(low, zero, q_).astype(bf16)

    def twice(ref, rows=slice(None)):
        v = ref[rows, :]
        return jnp.concatenate([v, v], axis=1)

    def outer_unit(k, d, slot_, bp):
        lref, rref, half = ((hl, r1f, 1), (hr, r1m, 0))[d]
        both = lref[pl.ds(pl.multiple_of(k * 128, 128), 128), :]
        lhs0 = jnp.concatenate([both[:, 0:128], both[:, 128:256]], axis=0)
        b0, b1 = 2 * bp, 2 * bp + 1
        rhs0 = jnp.concatenate([flat[half, b0], flat[half, b1]], axis=1)
        o0 = jnp.dot(lhs0, rhs0, preferred_element_type=f32).astype(bf16)
        rhs1 = jnp.concatenate([rref[b0], rref[b1]], axis=1)
        o1 = jnp.dot(both, rhs1, preferred_element_type=f32).astype(bf16)
        for e, b in enumerate((b0, b1)):
            rows = slice(b * 32, b * 32 + 32)
            lanes = slice(e * 128, e * 128 + 128)
            for i in range(8):
                pbuf[slot_, rows, i * 128 : i * 128 + 128] = o0[i * 32 : i * 32 + 32, lanes]
            for i in range(4):
                pbuf[slot_, rows, (8 + i) * 128 : (9 + i) * 128] = o1[i * 32 : i * 32 + 32, lanes]

    def project_chunk(k, d, slot_, n):
        cols = slice(n * 256, n * 256 + 256)
        z_ = jnp.dot((wf, wm)[d][...], pbuf[slot_, :, cols], preferred_element_type=f32)
        z_ = jnp.maximum(z_ + twice(bout_b), 0.0)
        zbuf[k, :, cols] = z_ if d == 0 else zbuf[k, :, cols] + z_

    def norm_chunk(k, n):
        pair = zbuf[k, :, n * 256 : n * 256 + 256]
        mean = jnp.mean(pair, axis=0, keepdims=True)
        cen = pair - mean
        var = jnp.mean(cen * cen, axis=0, keepdims=True)
        nbuf[n % 2] = (cen * lax.rsqrt(var + EPSILON) * twice(pg_b) + twice(pb_b)).astype(bf16)

    def up_chunk(n, part):
        rows = slice(part * 128, part * 128 + 128)
        hid = jnp.dot(wup[rows, :], nbuf[n % 2], preferred_element_type=f32)
        hbuf[n % 2, rows, :] = jnp.maximum(hid + twice(bup_b, rows), 0.0).astype(bf16)

    def down_chunk(k, n):
        upd = jnp.dot(wdn[...], hbuf[n % 2], preferred_element_type=f32)
        res = zbuf[k, :, n * 256 : n * 256 + 256] + upd + twice(bdn_b)
        for e in range(2):
            c = 2 * n + e
            t = res[:, e * 128 : e * 128 + 128].T.astype(bf16)
            for q_ in range(4):
                if c < 8:
                    out[c // 4, 4 * k + c % 4, 48 * q_ : 48 * q_ + 32, :] = t[32 * q_ : 32 * q_ + 32]
                else:
                    out[0, 4 * k + c - 8, 48 * q_ + 32 : 48 * q_ + 48, :] = t[16 * q_ : 16 * q_ + 16]
                    out[1, 4 * k + c - 8, 48 * q_ + 32 : 48 * q_ + 48, :] = t[64 + 16 * q_ : 80 + 16 * q_]

    def outer(k, d, slot_):
        return [functools.partial(outer_unit, k, d, slot_, bp) for bp in range(16)]

    def project(k, d, slot_):
        return [functools.partial(project_chunk, k, d, slot_, n) for n in range(6)]

    def transition(k):
        stages = []
        for n in range(0, 6, 2):
            both = (n, n + 1)
            stages += [functools.partial(norm_chunk, k, m) for m in both]
            for part in range(4):
                stages += [functools.partial(up_chunk, m, part) for m in both]
            stages += [functools.partial(down_chunk, k, m) for m in both]
        return stages

    def interleave(*lists):
        steps = [((i + 0.5) / len(l), j, f) for j, l in enumerate(lists) for i, f in enumerate(l)]
        for _, _, f in sorted(steps, key=lambda t: t[:2]):
            f()

    one = jnp.int32(1)
    shared(0).wait_recv()

    @pl.when(offset == 0)
    def _():
        make_rows(0)
        send_rows(0, hl, 0)
        send_rows(0, hl, one)

    for dz in (0, -1, 1, -2, 2):
        got_over(1, dz)
        share(1, 1 - ylo, dz)
    spread(0, r1m)

    @pl.when(offset == 0)
    def _():
        send_rows(0, hl, 2 * one)

    for dz in (-3, 3, -4):
        got_over(1, dz)
        share(1, 1 - ylo, dz)
    pass_root(0, hl, 0)
    pass_root(0, hl, one)
    shared(1).wait_recv()
    spread(1, r1f)

    @pl.when(offset == 0)
    def _():
        make_rows(1)

    def send_left(k):
        @pl.when(offset == 0)
        def _():
            send_rows(0, hl, k)

    def send_right(k):
        @pl.when(offset == 0)
        def _():
            send_rows(1, hr, k)

    pass_side(0, hl, 0)
    pass_side(0, hl, one)
    pass_far(0, hl, 0)
    send_left(3 * one)
    send_right(0 * one)
    interleave(outer(0, 0, 0))

    def left_step(k, parity):
        @pl.when(k < 5)
        def _():
            pass_root(0, hl, k + 1)
            pass_side(0, hl, k + 1)

        pass_far(0, hl, k)

        @pl.when(k < 3)
        def _():
            send_left(k + 3)

        send_right(k)

        @pl.when(k >= 2)
        def _():
            pass_root(1, hr, k - 2)

        @pl.when(k >= 4)
        def _():
            pass_side(1, hr, k - 4)

        interleave(outer(k, 0, parity), project(k - 1, 0, 1 - parity))

    def left_pair(t, carry):
        left_step(2 * t + 1, 1)
        left_step(2 * t + 2, 0)
        return carry

    lax.fori_loop(0, 2, left_pair, 0)
    left_step(jnp.int32(5), 1)

    pass_root(1, hr, 4 * one)
    pass_side(1, hr, 2 * one)
    pass_far(1, hr, 0 * one)
    interleave(outer(0, 1, 0), project(5, 0, 1))
    pass_root(1, hr, 5 * one)
    pass_side(1, hr, 3 * one)
    pass_far(1, hr, one)
    interleave(outer(1, 1, 1), project(0, 1, 0))

    def right_step(k, parity):
        @pl.when(k < 3)
        def _():
            pass_side(1, hr, k + 3)

        pass_far(1, hr, k + 1)
        interleave(outer(k + 1, 1, 1 - parity), project(k, 1, parity), transition(k - 1))

    def right_pair(t, carry):
        right_step(2 * t + 1, 1)
        right_step(2 * t + 2, 0)
        return carry

    lax.fori_loop(0, 2, right_pair, 0)
    interleave(project(5, 1, 1), transition(4))
    interleave(transition(5))

    for h, dst in ((0, hl), (1, hr)):
        for k in range(6):

            @pl.when(far_source)
            def _(h=h, dst=dst, k=k):
                first(h, dst, k).wait_send()

            @pl.when(offset == 0)
            def _(h=h, dst=dst, k=k):
                for way in range(3 if k + h == 0 else 2):
                    direct(h, dst, k, way).wait_send()

            if k + h > 0:

                @pl.when(offset == (1, 3)[k % 2])
                def _(h=h, dst=dst, k=k):
                    onward(h, dst, k, k % 2).wait_send()

    for h in range(2):
        shared(h).wait_send()
    for c in sent:
        c.wait_send()


def fused(x, *params):
    rows = x.shape[0]
    bf16, f32 = jnp.bfloat16, jnp.float32
    dma = pltpu.SemaphoreType.DMA
    args = (x,) + tuple(p[None, :] if p.ndim == 1 else p for p in params)
    args = tuple(pltpu.with_memory_space_constraint(a, pltpu.HBM) for a in args)
    out_bytes = 2 * 24 * 192 * 128 * 2
    out = pl.pallas_call(
        fused_kernel,
        in_specs=[pl.BlockSpec(memory_space=pltpu.HBM)] * len(args),
        out_specs=pl.BlockSpec(memory_space=pltpu.VMEM),
        out_shape=jax.ShapeDtypeStruct((2, 24, 192, 128), bf16),
        scratch_shapes=[pltpu.VMEM(a.shape, a.dtype) for a in args] + [
            dma((len(args),)),
            pltpu.VMEM((2, 48, 32, rows, 128), bf16),
            pltpu.VMEM((768, 256), bf16),
            pltpu.VMEM((768, 256), bf16),
            pltpu.VMEM((2, 48, rows, 128), f32),
            pltpu.VMEM((2, 48, rows, 128), bf16),
            pltpu.VMEM((2, 768, 128), f32),
            pltpu.VMEM((2, 768, 256), bf16),
            pltpu.VMEM((32, 256, 128), bf16),
            pltpu.VMEM((32, 256, 128), bf16),
            pltpu.VMEM((2, 1024, 1536), bf16),
            pltpu.VMEM((6, 128, 1536), f32),
            pltpu.VMEM((2, 128, 256), bf16),
            pltpu.VMEM((2, 512, 256), bf16),
            pltpu.VMEM((1024, 128), f32),
            pltpu.VMEM((128, 1024), bf16),
            pltpu.VMEM((128, 1024), bf16),
            pltpu.VMEM((512, 128), bf16),
            pltpu.VMEM((128, 512), bf16),
            pltpu.VMEM((128, 128), f32),
            pltpu.VMEM((128, 128), f32),
            pltpu.VMEM((128, 128), f32),
            pltpu.VMEM((128, 128), f32),
            pltpu.VMEM((512, 128), f32),
            dma((2,)),
            dma((8,)),
            dma((8,)),
            dma((2, 8)),
            dma((2, 8)),
            dma((2, 8)),
            dma((2, 8)),
            dma((2,)),
            dma((2,)),
            dma((2, 6)),
            dma((2, 3, 6)),
            dma((2, 6)),
        ],
        compiler_params=pltpu.CompilerParams(
            collective_id=0, has_side_effects=True, vmem_limit_bytes=48 * 1024 * 1024
        ),
        name="fused",
    )(*args)
    return out.reshape(48, 192, 128)


def shards(
    alignment,
    alignment_norm_gain,
    alignment_norm_bias,
    projection_weight,
    projection_bias_pair,
    *rest,
):
    return fused(
        alignment,
        alignment_norm_gain,
        alignment_norm_bias,
        projection_weight.T,
        projection_bias_pair,
        *rest,
    )


def solution(mesh):
    return jax.shard_map(
        shards,
        mesh=mesh,
        in_specs=(P("row", "col", None),) + (P(),) * 12,
        out_specs=P("row", "col", None),
        check_vma=False,
    )
```

```python
import functools

import jax
import jax.numpy as jnp
from jax import lax
from jax.experimental import pallas as pl
from jax.experimental.pallas import tpu as pltpu
from jax.sharding import PartitionSpec as P

EPSILON = 1e-05
VMEM_LIMIT = 60 * 1024 * 1024


MESH = pl.DeviceIdType.MESH
ZN, XN = 8, 4


def project_block(x_ref, gain_ref, bias_ref, w_ref, pbias_ref, stage):
    rows = x_ref.shape[0]
    low = lax.broadcasted_iota(jnp.int32, (1, 128), 1) < 64
    w2 = jnp.concatenate([w_ref[...], w_ref[...]], axis=0)
    pbias = jnp.concatenate([pbias_ref[...], pbias_ref[...]], axis=1)
    for s in range(rows):
        x = x_ref[s].astype(jnp.float32)
        mean = jnp.mean(x, axis=-1, keepdims=True)
        cen = x - mean
        var = jnp.mean(cen * cen, axis=-1, keepdims=True)
        normed = (cen * lax.rsqrt(var + EPSILON) * gain_ref[...] + bias_ref[...]).astype(jnp.bfloat16)
        d = lax.dot_general(normed, w2, (((1,), (1,)), ((), ())), preferred_element_type=jnp.float32)
        d = d + pbias
        t0 = jnp.concatenate([d[48 * q : 48 * q + 32] for q in range(4)], axis=0).T
        t1 = jnp.concatenate([d[48 * q + 32 : 48 * q + 48] for q in range(4)] * 2, axis=0).T
        for h in range(2):
            stage[h, 0:32, s, :] = t0[32 * h : 32 * h + 32]
            stage[h, 32:48, s, :] = jnp.where(low, t1[32 * h : 32 * h + 16], t1[32 * h + 16 : 32 * h + 32])


def fused_kernel(
    *refs,
):
    ins, vins = refs[:13], refs[14:27]
    out = refs[13]
    in_sem = refs[27]
    fetch = [pltpu.make_async_copy(a, v, in_sem.at[i]) for i, (a, v) in enumerate(zip(ins, vins))]
    for c in fetch:
        c.start()
    fused_body(fetch, *vins, out, *refs[28:])


def fused_body(
    fetch, x_ref, gain_ref, bias_ref, w_ref, pbias_ref, w_out, bout, pg, pb, w_up, bup, w_down, bdn, out,
    g, hl, hr, stage, block, hstage, hsend, r1f, r1m, pbuf, zbuf, nbuf, hbuf, wtmp,
    wf, wm, wup, wdn, bout_b, pg_b, pb_b, bdn_b, bup_b,
    own_sem, f_send, f_recv, z_send, z_recv, y_send, y_recv, p_send, p_recv, hs_sem, hf_sem, h_recv,
):
    bf16, f32 = jnp.bfloat16, jnp.float32

    def prepare_weights():
        total = 4 * 32
        wtmp[...] = w_out[...].astype(f32) * (1.0 / total)
        for m in range(8):
            rows = slice(m * 128, m * 128 + 128)
            wm[:, rows] = wtmp[rows, :].T.astype(bf16)
            picked = [wtmp[pl.ds(4 * m + e, 32, stride=32), :] for e in range(4)]
            wf[:, rows] = jnp.concatenate(picked, axis=0).T.astype(bf16)
        for m in range(4):
            rows = slice(m * 128, m * 128 + 128)
            wup[rows, :] = w_up[:, rows].astype(f32).T.astype(bf16)
            wdn[:, rows] = w_down[rows, :].astype(f32).T.astype(bf16)
            bup_b[rows, :] = jnp.broadcast_to(bup[:, rows], (128, 128)).T
        for wide, narrow in ((bout_b, bout), (pg_b, pg), (pb_b, pb), (bdn_b, bdn)):
            wide[...] = jnp.broadcast_to(narrow[...], (128, 128)).T

    row, col = lax.axis_index("row"), lax.axis_index("col")
    core = lax.rem(row, 2)
    z = lax.rem(row // 2, ZN)
    ylo = row // (2 * ZN)
    x = lax.rem(col, XN)
    yhi = col // XN

    def row_of(ylo_, z_, core_):
        return (ylo_ * ZN + z_) * 2 + core_

    zup, zdn = lax.rem(z + 1, ZN), lax.rem(z + ZN - 1, ZN)
    up = (row_of(ylo, zup, core), col)
    down = (row_of(ylo, zdn, core), col)
    across = (row_of(1 - ylo, z, core), col)
    partner = (row_of(ylo, z, 1 - core), col)
    xup = (row, yhi * XN + lax.rem(x + 1, XN))
    xdn = (row, yhi * XN + lax.rem(x + XN - 1, XN))
    facing = (row_of(1 - ylo, z, core), (1 - yhi) * XN + x)

    barrier = pltpu.get_barrier_semaphore()
    far = (row, yhi * XN + lax.rem(x + 2, XN))
    diagonal = [(facing[0], (1 - yhi) * XN + lax.rem(x + d, XN)) for d in range(1, XN)]
    near2 = [(row_of(ylo, lax.rem(z + d, ZN), core), col) for d in (2, ZN - 2)]
    others = (up, down, *near2, across, partner, xup, xdn, far, facing, *diagonal)
    for dev in others:
        pl.semaphore_signal(barrier, inc=1, device_id=dev, device_id_type=MESH)

    for c in fetch[:5]:
        c.wait()
    project_block(x_ref, gain_ref, bias_ref, w_ref, pbias_ref, stage)
    block[...] = stage[...].astype(bf16)
    own = [pltpu.make_async_copy(block.at[h], g.at[h, :, row], own_sem.at[h]) for h in range(2)]
    for c in own:
        c.start()
    pl.semaphore_wait(barrier, len(others))

    sent = []

    def slot(h, ylo_, dz, core_):
        return g.at[h, :, row_of(ylo_, lax.rem(z + dz + ZN, ZN), core_)]

    def copy(ref, send, recv, dev):
        c = pltpu.make_async_remote_copy(ref, ref, send, recv, device_id=dev, device_id_type=MESH)
        return c

    def send(ref, s, r, dev):
        c = copy(ref, s, r, dev)
        c.start()
        sent.append(c)

    def arrived(ref, r):
        copy(ref, own_sem.at[0], r, partner).wait_recv()

    up2 = (row_of(ylo, lax.rem(z + 2, ZN), core), col)
    down2 = (row_of(ylo, lax.rem(z + ZN - 2, ZN), core), col)

    def along(h, dz, there, dev):
        send(slot(h, ylo, dz, core), z_send.at[h, there + 4], z_recv.at[h, there + 4], dev)

    def got(h, dz):
        arrived(slot(h, ylo, dz, core), z_recv.at[h, dz + 4])

    def over(h, dz):
        send(slot(h, ylo, dz, core), y_send.at[h, dz + 4], y_recv.at[h, dz + 4], across)

    def got_over(h, dz):
        arrived(slot(h, 1 - ylo, dz, core), y_recv.at[h, dz + 4])

    def share(h, ylo_, dz):
        copy(slot(h, ylo_, dz, core), p_send.at[h], p_recv.at[h], partner).start()

    def shared(h):
        whole = g.at[h, 0:24]
        return copy(whole, p_send.at[h], p_recv.at[h], partner)

    own[0].wait()
    along(0, 0, -1, up)
    along(0, 0, 1, down)
    along(0, 0, -2, up2)
    along(0, 0, 2, down2)
    over(0, 0)
    share(0, ylo, 0)
    own[1].wait()
    along(1, 0, -1, up)
    along(1, 0, 1, down)
    share(1, ylo, 0)
    for c in fetch[5:]:
        c.wait()
    prepare_weights()
    for dz in (-1, 1):
        got(0, dz)
        over(0, dz)
        share(0, ylo, dz)
    got(0, -2)
    along(0, -2, -3, up)
    along(0, -2, -4, up2)
    over(0, -2)
    share(0, ylo, -2)
    got(0, 2)
    along(0, 2, 3, down)
    over(0, 2)
    share(0, ylo, 2)
    for dz in (-1, 1):
        got(1, dz)
        along(1, dz, dz * 2, up if dz < 0 else down)
        share(1, ylo, dz)
    for dz in (-3, 3, -4):
        got(0, dz)
        over(0, dz)
        share(0, ylo, dz)
    for dz in (0, -1, 1):
        over(1, dz)
    for dz in (-2, 2):
        got(1, dz)
        along(1, dz, dz * 3 // 2, up if dz < 0 else down)
        over(1, dz)
        share(1, ylo, dz)
    for dz in (0, -1, 1, -2, 2):
        got_over(0, dz)
        share(0, 1 - ylo, dz)
    got(1, -3)
    along(1, -3, -4, up)
    over(1, -3)
    share(1, ylo, -3)
    for dz in (-3, 3, -4):
        got_over(0, dz)
        share(0, 1 - ylo, dz)
    got(1, 3)
    over(1, 3)
    share(1, ylo, 3)
    got(1, -4)
    over(1, -4)
    share(1, ylo, -4)

    offset = lax.rem(x - z // 2 + XN, XN)
    q = lax.rem(row, 4)
    shift0 = lax.rem(128 - 32 * q, 128)
    shift1 = lax.rem(128 - 32 * q + 64, 128)
    shift2 = lax.rem(128 - 16 * q + 32, 128)
    lane = lax.broadcasted_iota(jnp.int32, (1, 128), 1)
    flat = g.reshape(2, 48, 128, 128)
    self_source = (offset == 0) & (ylo == yhi)
    far_source = (offset == 0) & (ylo != yhi)

    def chunk(ref, k):
        return ref.at[pl.ds(pl.multiple_of(k * 128, 128), 128)]

    def local(h, dst, k):
        return pltpu.make_async_copy(chunk(hsend.at[h], k), chunk(dst, k), h_recv.at[h, k])

    def first(h, dst, k):
        return pltpu.make_async_remote_copy(
            chunk(hsend.at[h], k), chunk(dst, k), hs_sem.at[h, k], h_recv.at[h, k], device_id=facing, device_id_type=MESH
        )

    def direct(h, dst, k, way):
        step_ = (1, XN - 1, 2)[way]
        dev = (jnp.where(ylo == yhi, row, facing[0]), jnp.where(ylo == yhi, yhi, 1 - yhi) * XN + lax.rem(x + step_, XN))
        return pltpu.make_async_remote_copy(
            chunk(hsend.at[h], k), chunk(dst, k), hf_sem.at[h, way, k], h_recv.at[h, k], device_id=dev, device_id_type=MESH
        )

    def onward(h, dst, k, way):
        return copy(chunk(dst, k), hf_sem.at[h, way, k], h_recv.at[h, k], (xup, xdn)[way])

    def make_rows(h):
        for p in range(16):
            a0 = pltpu.roll(flat[h, p].astype(f32), shift0, axis=1)
            a1 = pltpu.roll(flat[h, p + 16].astype(f32), shift1, axis=1)
            b = pltpu.roll(flat[h, 32 + p].astype(f32), shift2, axis=1)
            t = jnp.where(lane < 32, a0, jnp.where((lane >= 64) & (lane < 96), a1, b)).T
            for e in range(2):
                at = pl.ds(p + 16 * e, 24, stride=32)
                hstage[0, at, :] = t[64 * e : 64 * e + 24]
                hstage[1, at, :] = t[64 * e + 24 : 64 * e + 48]
        hsend[h, :, 0:128] = hstage[0].astype(bf16)
        hsend[h, :, 128:256] = hstage[1].astype(bf16)

    def send_rows(h, dst, k):
        @pl.when(self_source)
        def _():
            local(h, dst, k).start()
            direct(h, dst, k, 0).start()
            direct(h, dst, k, 1).start()

        @pl.when(far_source)
        def _():
            first(h, dst, k).start()

        if h == 0 and isinstance(k, int):

            @pl.when(offset == 0)
            def _():
                direct(h, dst, k, 2).start()

    def pass_root(h, dst, k):
        @pl.when(offset == 0)
        def _():
            local(h, dst, k).wait()

        @pl.when(far_source)
        def _():
            onward(h, dst, k, 0).start()
            onward(h, dst, k, 1).start()

    def pass_side(h, dst, k):
        @pl.when((offset == 1) | (offset == 3))
        def _():
            local(h, dst, k).wait()

        @pl.when((offset == 1) & (lax.rem(k, 2) == 0) & ((k > 0) | (h > 0)))
        def _():
            onward(h, dst, k, 0).start()

        @pl.when((offset == 3) & (lax.rem(k, 2) == 1))
        def _():
            onward(h, dst, k, 1).start()

    def pass_far(h, dst, k):
        @pl.when(offset == 2)
        def _():
            local(h, dst, k).wait()

    low = lane < 64
    zero = jnp.zeros((128, 128), f32)

    def spread(h, dst):
        for b in range(16):
            q_ = flat[h, 32 + b].astype(f32)
            r_ = pltpu.roll(q_, 64, axis=1)
            dst[b, 0:128] = jnp.where(low, q_, zero).astype(bf16)
            dst[b, 128:256] = jnp.where(low, zero, r_).astype(bf16)
            dst[b + 16, 0:128] = jnp.where(low, r_, zero).astype(bf16)
            dst[b + 16, 128:256] = jnp.where(low, zero, q_).astype(bf16)

    def twice(ref, rows=slice(None)):
        v = ref[rows, :]
        return jnp.concatenate([v, v], axis=1)

    def outer_unit(k, d, slot_, bp):
        lref, rref, half = ((hl, r1f, 1), (hr, r1m, 0))[d]
        both = lref[pl.ds(pl.multiple_of(k * 128, 128), 128), :]
        lhs0 = jnp.concatenate([both[:, 0:128], both[:, 128:256]], axis=0)
        b0, b1 = 2 * bp, 2 * bp + 1
        rhs0 = jnp.concatenate([flat[half, b0], flat[half, b1]], axis=1)
        o0 = jnp.dot(lhs0, rhs0, preferred_element_type=f32).astype(bf16)
        rhs1 = jnp.concatenate([rref[b0], rref[b1]], axis=1)
        o1 = jnp.dot(both, rhs1, preferred_element_type=f32).astype(bf16)
        for e, b in enumerate((b0, b1)):
            rows = slice(b * 32, b * 32 + 32)
            lanes = slice(e * 128, e * 128 + 128)
            for i in range(8):
                pbuf[slot_, rows, i * 128 : i * 128 + 128] = o0[i * 32 : i * 32 + 32, lanes]
            for i in range(4):
                pbuf[slot_, rows, (8 + i) * 128 : (9 + i) * 128] = o1[i * 32 : i * 32 + 32, lanes]

    def project_chunk(k, d, slot_, n):
        cols = slice(n * 256, n * 256 + 256)
        z_ = jnp.dot((wf, wm)[d][...], pbuf[slot_, :, cols], preferred_element_type=f32)
        z_ = jnp.maximum(z_ + twice(bout_b), 0.0)
        zbuf[k, :, cols] = z_ if d == 0 else zbuf[k, :, cols] + z_

    def norm_chunk(k, n):
        pair = zbuf[k, :, n * 256 : n * 256 + 256]
        mean = jnp.mean(pair, axis=0, keepdims=True)
        cen = pair - mean
        var = jnp.mean(cen * cen, axis=0, keepdims=True)
        nbuf[n % 2] = (cen * lax.rsqrt(var + EPSILON) * twice(pg_b) + twice(pb_b)).astype(bf16)

    def up_chunk(n, part):
        rows = slice(part * 128, part * 128 + 128)
        hid = jnp.dot(wup[rows, :], nbuf[n % 2], preferred_element_type=f32)
        hbuf[n % 2, rows, :] = jnp.maximum(hid + twice(bup_b, rows), 0.0).astype(bf16)

    def down_chunk(k, n):
        upd = jnp.dot(wdn[...], hbuf[n % 2], preferred_element_type=f32)
        res = zbuf[k, :, n * 256 : n * 256 + 256] + upd + twice(bdn_b)
        for e in range(2):
            c = 2 * n + e
            t = res[:, e * 128 : e * 128 + 128].T.astype(bf16)
            for q_ in range(4):
                if c < 8:
                    out[c // 4, 4 * k + c % 4, 48 * q_ : 48 * q_ + 32, :] = t[32 * q_ : 32 * q_ + 32]
                else:
                    out[0, 4 * k + c - 8, 48 * q_ + 32 : 48 * q_ + 48, :] = t[16 * q_ : 16 * q_ + 16]
                    out[1, 4 * k + c - 8, 48 * q_ + 32 : 48 * q_ + 48, :] = t[64 + 16 * q_ : 80 + 16 * q_]

    def outer(k, d, slot_):
        return [functools.partial(outer_unit, k, d, slot_, bp) for bp in range(16)]

    def project(k, d, slot_):
        return [functools.partial(project_chunk, k, d, slot_, n) for n in range(6)]

    def transition(k):
        stages = []
        for n in range(0, 6, 2):
            both = (n, n + 1)
            stages += [functools.partial(norm_chunk, k, m) for m in both]
            for part in range(4):
                stages += [functools.partial(up_chunk, m, part) for m in both]
            stages += [functools.partial(down_chunk, k, m) for m in both]
        return stages

    def interleave(*lists):
        steps = [((i + 0.5) / len(l), j, f) for j, l in enumerate(lists) for i, f in enumerate(l)]
        for _, _, f in sorted(steps, key=lambda t: t[:2]):
            f()

    one = jnp.int32(1)
    shared(0).wait_recv()

    @pl.when(offset == 0)
    def _():
        make_rows(0)
        send_rows(0, hl, 0)
        send_rows(0, hl, one)

    for dz in (0, -1, 1, -2, 2):
        got_over(1, dz)
        share(1, 1 - ylo, dz)
    spread(0, r1m)

    @pl.when(offset == 0)
    def _():
        send_rows(0, hl, 2 * one)

    pass_root(0, hl, 0)
    for dz in (-3, 3, -4):
        got_over(1, dz)
        share(1, 1 - ylo, dz)
    pass_root(0, hl, one)
    shared(1).wait_recv()
    spread(1, r1f)

    @pl.when(offset == 0)
    def _():
        make_rows(1)

    def send_left(k):
        @pl.when(offset == 0)
        def _():
            send_rows(0, hl, k)

    def send_right(k):
        @pl.when(offset == 0)
        def _():
            send_rows(1, hr, k)

    pass_side(0, hl, 0)
    pass_side(0, hl, one)
    pass_far(0, hl, 0)
    send_left(3 * one)
    send_right(0 * one)
    interleave(outer(0, 0, 0))

    def left_step(k, parity):
        @pl.when(k < 5)
        def _():
            pass_root(0, hl, k + 1)
            pass_side(0, hl, k + 1)

        pass_far(0, hl, k)

        @pl.when(k < 3)
        def _():
            send_left(k + 3)

        send_right(k)

        @pl.when(k >= 2)
        def _():
            pass_root(1, hr, k - 2)

        @pl.when(k >= 4)
        def _():
            pass_side(1, hr, k - 4)

        interleave(outer(k, 0, parity), project(k - 1, 0, 1 - parity))

    def left_pair(t, carry):
        left_step(2 * t + 1, 1)
        left_step(2 * t + 2, 0)
        return carry

    lax.fori_loop(0, 2, left_pair, 0)
    left_step(jnp.int32(5), 1)

    pass_root(1, hr, 4 * one)
    pass_side(1, hr, 2 * one)
    pass_far(1, hr, 0 * one)
    interleave(outer(0, 1, 0), project(5, 0, 1))
    pass_root(1, hr, 5 * one)
    pass_side(1, hr, 3 * one)
    pass_far(1, hr, one)
    interleave(outer(1, 1, 1), project(0, 1, 0))

    def right_step(k, parity):
        @pl.when(k < 3)
        def _():
            pass_side(1, hr, k + 3)

        pass_far(1, hr, k + 1)
        interleave(outer(k + 1, 1, 1 - parity), project(k, 1, parity), transition(k - 1))

    def right_pair(t, carry):
        right_step(2 * t + 1, 1)
        right_step(2 * t + 2, 0)
        return carry

    lax.fori_loop(0, 2, right_pair, 0)
    interleave(project(5, 1, 1), transition(4))
    interleave(transition(5))

    for h, dst in ((0, hl), (1, hr)):
        for k in range(6):

            @pl.when(far_source)
            def _(h=h, dst=dst, k=k):
                first(h, dst, k).wait_send()

            @pl.when(offset == 0)
            def _(h=h, dst=dst, k=k):
                for way in range(3 if k + h == 0 else 2):
                    direct(h, dst, k, way).wait_send()

            if k + h > 0:

                @pl.when(offset == (1, 3)[k % 2])
                def _(h=h, dst=dst, k=k):
                    onward(h, dst, k, k % 2).wait_send()

    for h in range(2):
        shared(h).wait_send()
    for c in sent:
        c.wait_send()


def fused(x, *params):
    rows = x.shape[0]
    bf16, f32 = jnp.bfloat16, jnp.float32
    dma = pltpu.SemaphoreType.DMA
    args = (x,) + tuple(p[None, :] if p.ndim == 1 else p for p in params)
    args = tuple(pltpu.with_memory_space_constraint(a, pltpu.HBM) for a in args)
    out_bytes = 2 * 24 * 192 * 128 * 2
    out = pl.pallas_call(
        fused_kernel,
        in_specs=[pl.BlockSpec(memory_space=pltpu.HBM)] * len(args),
        out_specs=pl.BlockSpec(memory_space=pltpu.VMEM),
        out_shape=jax.ShapeDtypeStruct((2, 24, 192, 128), bf16),
        scratch_shapes=[pltpu.VMEM(a.shape, a.dtype) for a in args] + [
            dma((len(args),)),
            pltpu.VMEM((2, 48, 32, rows, 128), bf16),
            pltpu.VMEM((768, 256), bf16),
            pltpu.VMEM((768, 256), bf16),
            pltpu.VMEM((2, 48, rows, 128), f32),
            pltpu.VMEM((2, 48, rows, 128), bf16),
            pltpu.VMEM((2, 768, 128), f32),
            pltpu.VMEM((2, 768, 256), bf16),
            pltpu.VMEM((32, 256, 128), bf16),
            pltpu.VMEM((32, 256, 128), bf16),
            pltpu.VMEM((2, 1024, 1536), bf16),
            pltpu.VMEM((6, 128, 1536), f32),
            pltpu.VMEM((2, 128, 256), bf16),
            pltpu.VMEM((2, 512, 256), bf16),
            pltpu.VMEM((1024, 128), f32),
            pltpu.VMEM((128, 1024), bf16),
            pltpu.VMEM((128, 1024), bf16),
            pltpu.VMEM((512, 128), bf16),
            pltpu.VMEM((128, 512), bf16),
            pltpu.VMEM((128, 128), f32),
            pltpu.VMEM((128, 128), f32),
            pltpu.VMEM((128, 128), f32),
            pltpu.VMEM((128, 128), f32),
            pltpu.VMEM((512, 128), f32),
            dma((2,)),
            dma((8,)),
            dma((8,)),
            dma((2, 8)),
            dma((2, 8)),
            dma((2, 8)),
            dma((2, 8)),
            dma((2,)),
            dma((2,)),
            dma((2, 6)),
            dma((2, 3, 6)),
            dma((2, 6)),
        ],
        compiler_params=pltpu.CompilerParams(
            collective_id=0, has_side_effects=True, vmem_limit_bytes=48 * 1024 * 1024
        ),
        name="fused",
    )(*args)
    return out.reshape(48, 192, 128)


def shards(
    alignment,
    alignment_norm_gain,
    alignment_norm_bias,
    projection_weight,
    projection_bias_pair,
    *rest,
):
    return fused(
        alignment,
        alignment_norm_gain,
        alignment_norm_bias,
        projection_weight.T,
        projection_bias_pair,
        *rest,
    )


def solution(mesh):
    return jax.shard_map(
        shards,
        mesh=mesh,
        in_specs=(P("row", "col", None),) + (P(),) * 12,
        out_specs=P("row", "col", None),
        check_vma=False,
    )
```
